32 devices in a mesh: dp: 4 (over y, x), ctx: 8 (over z, core).
Axes of the slice: x: 2, y: 2, z: 4, core: 2. Of those that a mesh axis runs over, the one named last changes fastest.
Arguments:
- queries: bfloat16 [4096, 64, 128], P(('dp', 'ctx')), parts along dimension 0, may hold values from -4.5 to 4.5
- keys: bfloat16 [4096, 8, 128], P(('dp', 'ctx')), parts along dimension 0, may hold values from -4.5 to 4.5
- values: bfloat16 [4096, 8, 128], P(('dp', 'ctx')), parts along dimension 0, may hold values from -6 to 6
- out_grad: bfloat16 [4096, 64, 128], P(('dp', 'ctx')), parts along dimension 0, may hold values from -48 to 48
- rand_blocks: int32 [256, 16, 3], P(('dp', 'ctx')), parts along dimension 0, may hold values from 0 to 15, as said below
- global_blocks: int32 [8], P('dp'), parts along dimension 0, may hold values from 0 to 15, as said below
Outputs:
- output: bfloat16 [4096, 64, 128], P(('dp', 'ctx')), parts along dimension 0
- query_grad: bfloat16 [4096, 64, 128], P(('dp', 'ctx')), parts along dimension 0
- key_grad: bfloat16 [4096, 8, 128], P(('dp', 'ctx')), parts along dimension 0
- value_grad: bfloat16 [4096, 8, 128], P(('dp', 'ctx')), parts along dimension 0
The draws below stay inside these ranges and needn't reach their ends.
There are 4 independent parts, one for each index of `dp`. The reference program is written for one: setup_inputs(seed, part) draws one part's arguments, and reference() takes and returns one part's arrays. A program takes and returns all parts, laid end to end along the dimension named above; each array names one. Nothing has to cross between parts.
Inputs may be any that keep to these rules, and one draw needn't show every extreme that they name: `rand_blocks`: for each query head and query block, 3 different blocks, none of them the query block or a block beside it (modulo 16), none of them a global block. `global_blocks`: 2 different blocks.
All inputs are finite; a program needn't handle non-finite values.
Results may differ from the reference program's by a relative error of at most 0.011.
Values may be sent and summed in bfloat16 or wider, within the bound.
A program may use at most 192 MiB of HBM per device.

```python
import math
import jax
import jax.numpy as jnp
from jax import lax

H = 64
KVH = 8
DH = 128
BLK = 64
GLOB = 2
RAND = 3
LEN = 1024
NB = 16


def pick_globals(key):
    order = jax.random.permutation(jax.random.fold_in(key, 11), NB)
    return order[:GLOB].astype(jnp.int32)


def draw_global_blocks(key, part):
    return pick_globals(key)


def draw_rand_blocks(key, part):
    glob_ids = pick_globals(key)
    block_ids = jnp.arange(NB, dtype=jnp.int32)
    distance = (block_ids[None, :] - block_ids[:, None]) % NB
    banned = jnp.logical_or(distance <= 1, distance == NB - 1)
    is_global = jnp.any(block_ids[:, None] == glob_ids[None, :], axis=1)
    banned = jnp.logical_or(banned, is_global[None, :])
    noise = jax.random.randint(jax.random.fold_in(key, 17), (H, NB, NB), 0, 262144)
    ranked = noise * 4096 + block_ids[None, None, :]
    ranked = jnp.where(banned[None, :, :], -1 - block_ids[None, None, :], ranked)
    picked = lax.top_k(ranked, RAND)[1]
    return picked.astype(jnp.int32)


def draw_queries(key, part):
    query_vals = jnp.clip(jax.random.normal(jax.random.fold_in(key, 23), (LEN, H, DH), jnp.float32), -4.0, 4.0)
    return query_vals.astype(jnp.bfloat16)


def draw_keys(key, part):
    key_vals = jnp.clip(jax.random.normal(jax.random.fold_in(key, 31), (LEN, KVH, DH), jnp.float32), -4.0, 4.0)
    return key_vals.astype(jnp.bfloat16)


def block_levels(key, extent, split, smallest, largest):
    level = 1.0
    for position, blocks in split:
        draws = jax.random.uniform(jax.random.fold_in(jax.random.fold_in(key, 6), position), (blocks,), jnp.float32, smallest / len(split), largest / len(split))
        level = level * jnp.repeat(jnp.exp(draws), extent[position] // blocks).reshape((-1,) + (1,) * (len(extent) - 1 - position))
    return level


def scatter_about(rng, extent, spread, bound, pieces=(), kind=jnp.bfloat16):
    values = jax.random.normal(rng, extent, jnp.float32) * spread
    if len(pieces) > 0:
        values = block_levels(rng, extent, pieces, -0.22, 0.18) * values
    return jnp.clip(values, min=-bound, max=bound).astype(kind)


def setup_inputs(seed: int = 0, part: int = 0) -> dict:
    key_of = jax.random.split(jax.random.key(seed), 7)
    part_splits = jax.random.split(jax.random.fold_in(key_of[6], part), 7)
    return {
        "queries": draw_queries(jax.random.fold_in(jax.random.fold_in(key_of[6], part), 71), part),
        "keys": draw_keys(jax.random.fold_in(jax.random.fold_in(key_of[6], part), 71), part),
        "values": scatter_about(part_splits[2], (LEN, KVH, DH), 1.0, 6.0, ((0, 8),)),
        "out_grad": scatter_about(part_splits[3], (LEN, H, DH), 8.0, 48.0, ((0, 8),)),
        "rand_blocks": draw_rand_blocks(jax.random.fold_in(jax.random.fold_in(key_of[6], part), 71), part),
        "global_blocks": draw_global_blocks(jax.random.fold_in(jax.random.fold_in(key_of[6], part), 71), part),
    }


def block_table(rand_head, global_blocks, block_count):
    row_ids = jnp.arange(block_count, dtype=jnp.int32)
    window = jnp.stack([(row_ids + block_count - 1) % block_count, row_ids, (row_ids + 1) % block_count], axis=1)
    glob_cols = jnp.broadcast_to(global_blocks.astype(jnp.int32)[None, :], (block_count, global_blocks.shape[0]))
    key_table = jnp.concatenate([window, glob_cols, rand_head.astype(jnp.int32)], axis=1)
    slot_count = key_table.shape[1]
    repeated = key_table[:, :, None] == key_table[:, None, :]
    earlier = jnp.arange(slot_count)[None, :] < jnp.arange(slot_count)[:, None]
    usable = jnp.logical_not(jnp.any(jnp.logical_and(repeated, earlier[None, :, :]), axis=2))
    return (key_table, usable)

def group_size(block_count, block_rows):
    return math.gcd(block_count, max(1, 512 // block_rows))

def contract(form, left, right):
    return jnp.einsum(form, left.astype(jnp.float32), right.astype(jnp.float32))

def forward_head(global_blocks, operands):
    query_h, key_h, value_h, rand_head = operands
    length, head_width = query_h.shape
    block_count = length // BLK
    per_step = group_size(block_count, BLK)
    step_count = block_count // per_step
    key_table, usable = block_table(rand_head, global_blocks, block_count)
    factor = 1.0 / math.sqrt(head_width)
    key_blocks = key_h.reshape(block_count, BLK, head_width)
    value_blocks = value_h.reshape(block_count, BLK, head_width)
    packs = (query_h.reshape(step_count, per_step, BLK, head_width), key_table.reshape(step_count, per_step, -1), usable.reshape(step_count, per_step, -1))

    def one_group(group_pack):
        query_g, table_g, usable_g = group_pack
        key_g = key_blocks[table_g].reshape(per_step, -1, head_width)
        value_g = value_blocks[table_g].reshape(per_step, -1, head_width)
        scores = contract('abd,akd->abk', query_g, key_g) * factor
        live_cols = jnp.repeat(usable_g, BLK, axis=1)[:, None, :]
        scores = jnp.where(live_cols, scores, -jnp.inf)
        row_max = lax.optimization_barrier(jnp.max(scores, axis=2, keepdims=True))
        raw_weight = jnp.exp(scores - row_max)
        prob_rows = (raw_weight / lax.optimization_barrier(jnp.sum(raw_weight, axis=2, keepdims=True))).astype(jnp.bfloat16)
        result = contract('abk,akd->abd', prob_rows, value_g).astype(jnp.bfloat16)
        return (result, prob_rows)
    result, prob_rows = lax.map(one_group, packs)
    return (result.reshape(length, head_width), prob_rows)

def backward_head(global_blocks, operands):
    query_h, key_h, value_h, grad_h, out_h, prob_all, rand_head = operands
    length, head_width = query_h.shape
    block_count = length // BLK
    per_step = group_size(block_count, BLK)
    step_count = block_count // per_step
    key_table, usable = block_table(rand_head, global_blocks, block_count)
    factor = 1.0 / math.sqrt(head_width)
    key_blocks = key_h.reshape(block_count, BLK, head_width)
    value_blocks = value_h.reshape(block_count, BLK, head_width)
    delta_all = lax.optimization_barrier(jnp.sum(grad_h.astype(jnp.float32) * out_h.astype(jnp.float32), axis=1))
    packs = (query_h.reshape(step_count, per_step, BLK, head_width), grad_h.reshape(step_count, per_step, BLK, head_width), delta_all.reshape(step_count, per_step, BLK), prob_all, key_table.reshape(step_count, per_step, -1))

    def one_group(carry, group_pack):
        key_acc, value_acc = carry
        query_g, grad_g, delta_g, prob_g, table_g = group_pack
        key_g = key_blocks[table_g].reshape(per_step, -1, head_width)
        value_g = value_blocks[table_g].reshape(per_step, -1, head_width)
        value_part = contract('abk,abd->akd', prob_g, grad_g)
        dprob = contract('abd,akd->abk', grad_g, value_g)
        dscore = (prob_g.astype(jnp.float32) * (dprob - delta_g[:, :, None])).astype(jnp.bfloat16)
        query_grad = (contract('abk,akd->abd', dscore, key_g) * factor).astype(jnp.bfloat16)
        key_part = contract('abk,abd->akd', dscore, query_g) * factor
        flat_ids = table_g.reshape(-1)
        key_acc = key_acc.at[flat_ids].add(key_part.reshape(-1, BLK, head_width))
        value_acc = value_acc.at[flat_ids].add(value_part.reshape(-1, BLK, head_width))
        return ((key_acc, value_acc), query_grad)
    zeros_acc = jnp.zeros((block_count, BLK, head_width), jnp.float32)
    (key_acc, value_acc), query_grad = lax.scan(one_group, (zeros_acc, zeros_acc), packs)
    return (query_grad.reshape(length, head_width), key_acc.reshape(length, head_width).astype(jnp.bfloat16), value_acc.reshape(length, head_width).astype(jnp.bfloat16))

def reference(queries, keys, values, out_grad, rand_blocks, global_blocks):
    heads_per_kv = H // KVH
    keys_wide = jnp.repeat(keys, heads_per_kv, axis=1)
    values_wide = jnp.repeat(values, heads_per_kv, axis=1)

    def per_head(head_pack):
        query_h, key_h, value_h, grad_h, rand_head = head_pack
        out_h, prob_all = forward_head(global_blocks, (query_h, key_h, value_h, rand_head))
        grads = backward_head(global_blocks, (query_h, key_h, value_h, grad_h, out_h, prob_all, rand_head))
        return (out_h, grads[0], grads[1], grads[2])
    out_all, query_all, key_parts, value_parts = lax.map(per_head, (jnp.moveaxis(queries, 1, 0), jnp.moveaxis(keys_wide, 1, 0), jnp.moveaxis(values_wide, 1, 0), jnp.moveaxis(out_grad, 1, 0), rand_blocks))
    output = jnp.moveaxis(out_all, 0, 1)
    query_grad = jnp.moveaxis(query_all, 0, 1)
    key_sum = key_parts.reshape(KVH, heads_per_kv, LEN, DH).astype(jnp.float32).sum(axis=1).astype(jnp.bfloat16)
    value_sum = value_parts.reshape(KVH, heads_per_kv, LEN, DH).astype(jnp.float32).sum(axis=1).astype(jnp.bfloat16)
    return (output, query_grad, jnp.moveaxis(key_sum, 0, 1), jnp.moveaxis(value_sum, 0, 1))
```

```python
import functools
import math

import jax
import jax.numpy as jnp
from jax import lax
from jax.experimental import pallas as pl
from jax.experimental.pallas import tpu as pltpu
from jax.sharding import PartitionSpec as P

BLK = 64
NT = (((1,), (1,)), ((), ()))
NN = (((1,), (0,)), ((), ()))


def dot(left, right, dims=NN):
    return lax.dot_general(left, right, dims, preferred_element_type=jnp.float32)


def flat_rows(block):
    rows = block.shape[0] * block.shape[1]
    return block.astype(jnp.float32).reshape(rows, block.shape[2])


def for_chunks(count, step, init):
    return lax.fori_loop(0, count, step, init, unroll=count <= 4)


def attention(geometry, q_ref, g_ref, kv_ref, bias_ref, out_ref, dq_ref, dkv_ref, s_buf, e_buf, acc):
    chunk, row_tile = geometry
    shards, _, _, shard_tokens, width = kv_ref.shape
    length = shards * shard_tokens
    count = length // chunk
    tokens, group, _ = q_ref.shape
    rows = tokens * group
    tiles = rows // row_tile
    tile_tokens = row_tile // group
    factor = 1.0 / math.sqrt(width)
    to_log2 = factor * math.log2(math.e)
    per_chunk = chunk // shard_tokens

    def kv_chunk(which, c):
        return kv_ref[pl.ds(c * per_chunk, per_chunk), 0, which].reshape(chunk, width)

    for tile in range(tiles):
        t0 = tile * tile_tokens
        lanes = pl.ds(tile * row_tile, row_tile)
        q = flat_rows(q_ref[pl.ds(t0, tile_tokens)]).astype(jnp.bfloat16)
        g32 = flat_rows(g_ref[pl.ds(t0, tile_tokens)])

        def score_step(c, top):
            s = dot(kv_chunk(0, c), q, NT) * to_log2
            blocks = chunk // BLK
            bias = bias_ref[0, pl.ds(c * blocks, blocks), :, lanes]
            s = (s.reshape(blocks, BLK, row_tile) + bias).reshape(chunk, row_tile)
            s_buf[pl.ds(c * chunk, chunk)] = s
            return jnp.maximum(top, jnp.max(s, axis=0, keepdims=True))

        top = for_chunks(count, score_step, jnp.full((1, row_tile), -jnp.inf, jnp.float32))

        def weight_step(c, carry):
            total, out_t = carry
            e = jnp.exp2(s_buf[pl.ds(c * chunk, chunk)] - top)
            total = total + jnp.sum(e, axis=0, keepdims=True)
            e16 = e.astype(jnp.bfloat16)
            e_buf[pl.ds(c * chunk, chunk)] = e16
            out_t = out_t + dot(kv_chunk(1, c).T, e16)
            return total, out_t

        total, out_t = for_chunks(
            count,
            weight_step,
            (jnp.zeros((1, row_tile), jnp.float32), jnp.zeros((width, row_tile), jnp.float32)),
        )
        inverse = 1.0 / total
        out16 = (out_t * inverse).T.astype(jnp.bfloat16)
        out32 = out16.astype(jnp.float32)
        out_ref[pl.ds(t0, tile_tokens)] = out32.reshape(tile_tokens, group, width).astype(jnp.bfloat16)
        delta = jnp.sum((g32 * out32).T, axis=0, keepdims=True) * inverse
        g16 = (g32.T * inverse).T.astype(jnp.bfloat16)

        def grad_step(c, dq_t):
            at = pl.ds(c * chunk, chunk)
            e16 = e_buf[at]
            dp = dot(kv_chunk(1, c), g16, NT)
            ds = (e16.astype(jnp.float32) * (dp - delta)).astype(jnp.bfloat16)
            dk = dot(ds, q)
            dv = dot(e16, g16)
            if tile > 0:
                dk = dk + acc[0, at]
                dv = dv + acc[1, at]
            if tile < tiles - 1:
                acc[0, at] = dk
                acc[1, at] = dv
            else:
                shape = (per_chunk, shard_tokens, width)
                spot = pl.ds(c * per_chunk, per_chunk)
                dkv_ref[spot, 0, 0] = (dk * factor).astype(jnp.bfloat16).reshape(shape)
                dkv_ref[spot, 0, 1] = dv.astype(jnp.bfloat16).reshape(shape)
            return dq_t + dot(kv_chunk(0, c).T, ds)

        dq_t = for_chunks(count, grad_step, jnp.zeros((width, row_tile), jnp.float32))
        dq = (dq_t * factor).T.reshape(tile_tokens, group, width)
        dq_ref[pl.ds(t0, tile_tokens)] = dq.astype(jnp.bfloat16)


def local_attention(queries, out_grad, kv, bias):
    tokens, heads, width = queries.shape
    shards, kv_heads, _, shard_tokens, _ = kv.shape
    group = heads // kv_heads
    length = shards * shard_tokens
    rows = tokens * group
    chunk = math.gcd(length, 256)
    row_tile = rows
    while row_tile * length > (1 << 21) and row_tile > 128:
        row_tile //= 2
    acc_rows = length if row_tile < rows else 8
    blocks = length // BLK
    q_spec = pl.BlockSpec((tokens, group, width), lambda g: (0, g, 0))
    kv_spec = pl.BlockSpec((shards, 1, 2, shard_tokens, width), lambda g: (0, g, 0, 0, 0))
    return pl.pallas_call(
        functools.partial(attention, (chunk, row_tile)),
        grid=(kv_heads,),
        in_specs=[
            q_spec,
            q_spec,
            kv_spec,
            pl.BlockSpec((1, blocks, 1, rows), lambda g: (g, 0, 0, 0)),
        ],
        out_specs=[q_spec, q_spec, kv_spec],
        out_shape=[
            jax.ShapeDtypeStruct(queries.shape, jnp.bfloat16),
            jax.ShapeDtypeStruct(queries.shape, jnp.bfloat16),
            jax.ShapeDtypeStruct(kv.shape, jnp.bfloat16),
        ],
        scratch_shapes=[
            pltpu.VMEM((length, row_tile), jnp.float32),
            pltpu.VMEM((length, row_tile), jnp.bfloat16),
            pltpu.VMEM((2, acc_rows, width), jnp.float32),
        ],
        compiler_params=pltpu.CompilerParams(vmem_limit_bytes=60 * 1024 * 1024),
        name="attention",
    )(queries, out_grad, kv, bias)


def row_bias(rand_all, global_blocks, first, here, block_count, kv_heads):
    heads = rand_all.shape[0]
    group = heads // kv_heads
    mine = lax.dynamic_slice_in_dim(rand_all, first, here, axis=1)
    ids = first + jnp.arange(here, dtype=jnp.int32)
    key_ids = jnp.arange(block_count, dtype=jnp.int32)
    away = (key_ids[None, :] - ids[:, None] + block_count + 1) % block_count
    common = (away <= 2) | jnp.any(key_ids[None, :, None] == global_blocks[None, None, :], axis=2)
    chosen = jnp.any(mine[:, :, None, :] == key_ids[None, None, :, None], axis=3)
    live = chosen | common[None]
    bias = jnp.where(live, 0.0, -jnp.inf).astype(jnp.float32)
    bias = bias.reshape(kv_heads, group, here, block_count).transpose(0, 3, 2, 1)
    bias = jnp.broadcast_to(bias[:, :, :, None, :], (kv_heads, block_count, here, BLK, group))
    return bias.reshape(kv_heads, block_count, 1, here * BLK * group)


def fused_kernel(
    rand_in, glob_in, k_in, v_in, q_hbm, g_hbm, out_ref, dq_ref, dk_ref, dv_ref,
    grads_ref, q_buf, g_buf, kv_buf, part_buf, sib_in, right_in, left_in, right_out, left_out,
    ids_out, ids_buf, bias_buf, s_buf, e_buf, ds_buf, vt_buf, kt_buf, qt_buf, gt_buf,
    q_sem, g_sem,
    ids_send, sib_send, fwd_send, back_send, pair_send, right_send, left_send,
    ids_recv, sib_recv, kv_recv, pair_recv, right_recv, left_recv,
):
    heads, _, chips, _, shard_tokens, width = kv_buf.shape
    shards = 2 * chips
    _, tokens, group, _ = q_buf.shape
    rows = tokens * group
    here = tokens // BLK
    block_count = shards * here
    lane_keys = chips * shard_tokens
    tile = 256
    tiles = rows // tile
    tile_tokens = tile // group
    chunk = 2 * shard_tokens
    chunks = shards * shard_tokens // chunk
    factor = 1.0 / math.sqrt(width)
    to_log2 = factor * math.log2(math.e)
    me = lax.axis_index("ctx")
    z, core = me // 2, me % 2
    pair = z * 2 + 1 - core
    ahead, behind = me + 2, me - 2
    last = chips - 1

    barrier = pltpu.get_barrier_semaphore()
    for k in range(1, shards):
        pl.semaphore_signal(
            barrier, inc=1, device_id={"ctx": lax.rem(me + k, shards)}, device_id_type=pl.DeviceIdType.MESH
        )

    def send(source, target, send_sem, recv_sem, to):
        return pltpu.make_async_remote_copy(
            src_ref=source, dst_ref=target, send_sem=send_sem, recv_sem=recv_sem,
            device_id={"ctx": to}, device_id_type=pl.DeviceIdType.MESH,
        )

    def send_ids(k):
        to = lax.rem(me + k, shards)
        return send(ids_out.at[to], ids_buf.at[me], ids_send, ids_recv.at[me], to)

    def got_ids(k):
        origin = lax.rem(me + k, shards)
        return send(ids_out.at[origin], ids_buf.at[origin], ids_send, ids_recv.at[origin], origin)

    def kv_move(h, origin, send_sem, to):
        spot = kv_buf.at[h, core, origin]
        return send(spot, spot, send_sem, kv_recv.at[h, origin], to)

    def right_kv(h, origin):
        return kv_move(h, origin, fwd_send, ahead)

    def left_kv(h, origin):
        return kv_move(h, origin, back_send, behind)

    def sib_kv(h, origin):
        spot = kv_buf.at[h, core, origin]
        return send(spot, spot, sib_send, sib_recv.at[h], pair)

    def pair_move(h, w):
        return send(part_buf.at[h, w, 1 - core], sib_in.at[h, w], pair_send, pair_recv.at[h, w], pair)

    def side_move(side, h, w, zd):
        if side == 0:
            return send(right_out.at[h, w, zd], right_in.at[h, w, zd], right_send, right_recv.at[h, w, zd], ahead)
        return send(left_out.at[h, w, zd], left_in.at[h, w, zd], left_send, left_recv.at[h, w, zd], behind)

    def head_columns(ref, h):
        return ref.at[:, pl.ds(pl.multiple_of(h * group, group), group), :]

    def load_q(h):
        return pltpu.make_async_copy(head_columns(q_hbm, h), q_buf.at[h], q_sem.at[h])

    def load_g(h):
        return pltpu.make_async_copy(head_columns(g_hbm, h), g_buf.at[h], g_sem.at[h])

    def each_head(step):
        def run(h, carry):
            step(h)
            return carry
        lax.fori_loop(0, heads, run, 0)

    for which, ref in enumerate((k_in, v_in)):
        turned = jnp.swapaxes(ref[...].astype(jnp.float32), 0, 1)
        kv_buf[:, core, z, which] = turned.astype(jnp.bfloat16)

    slots = rand_in.shape[0]
    lanes = ids_buf.shape[2]
    spread = lax.broadcasted_iota(jnp.int32, (group, lanes), 1) % group
    spread = (spread == lax.broadcasted_iota(jnp.int32, (group, lanes), 0)).astype(jnp.float32)
    for k in range(slots):
        picks = lax.dot_general(
            rand_in[k].astype(jnp.float32), spread, (((0,), (0,)), ((), ())), preferred_element_type=jnp.float32
        )
        for to in range(shards):
            for b in range(here):
                spot = to * here + b
                ids_out[to, b * slots + k:b * slots + k + 1] = picks[spot:spot + 1]
    ids_buf[me] = ids_out[me]

    pl.semaphore_wait(barrier, shards - 1)

    def own_right(h):
        @pl.when(z < last)
        def _():
            right_kv(h, z).start()

    def own_left(h):
        @pl.when(z > 0)
        def _():
            left_kv(h, z).start()

    def own_sib(h):
        sib_kv(h, z).start()

    def arrive(h, distance):
        for zz in range(chips):
            @pl.when(jnp.logical_and(z == zz, h < heads))
            def _(zz=zz):
                for origin in (zz - distance, zz + distance):
                    if origin < 0 or origin > last:
                        continue
                    kv_move(h, origin, fwd_send, pair).wait_recv()
                    if origin < zz < last:
                        right_kv(h, origin).start()
                    if 0 < zz < origin:
                        left_kv(h, origin).start()
                    sib_kv(h, origin).start()

    def over(low, high, step):
        def run(h, carry):
            step(h)
            return carry
        lax.fori_loop(low, high, run, 0)

    def combined(h, w, zd):
        return part_buf[h, w, core, zd].astype(jnp.float32) + sib_in[h, w, zd].astype(jnp.float32)

    def reduce(rank, h, w):
        for side in range(2):
            zz = rank if side == 0 else last - rank
            targets = range(last, zz, -1) if side == 0 else range(zz)
            out, arrived = (right_out, right_in) if side == 0 else (left_out, left_in)

            @pl.when(jnp.logical_and(z == zz, h >= 0))
            def _(side=side, targets=targets, out=out, arrived=arrived):
                for zd in targets:
                    total = combined(h, w, zd)
                    if rank > 0:
                        side_move(side, h, w, zd).wait_recv()
                        total = total + arrived[h, w, zd].astype(jnp.float32)
                    out[h, w, zd] = total.astype(jnp.bfloat16)
                    side_move(side, h, w, zd).start()

    def finish(h, w):
        for zz in range(chips):
            @pl.when(z == zz)
            def _(zz=zz):
                total = combined(h, w, zz)
                if zz > 0:
                    side_move(0, h, w, zz).wait_recv()
                    total = total + right_in[h, w, zz].astype(jnp.float32)
                if zz < last:
                    side_move(1, h, w, zz).wait_recv()
                    total = total + left_in[h, w, zz].astype(jnp.float32)
                grads_ref[h, w] = total.T.astype(jnp.bfloat16)

    def compute(h, hooks):
        load_q(h).wait()
        load_g(h).wait()
        ids = ids_buf[h]
        key_ids = lax.broadcasted_iota(jnp.int32, (block_count, lanes), 0)
        key_float = key_ids.astype(jnp.float32)
        for b in range(here):
            away = key_ids - (me * here + b) + (block_count + 1)
            for _ in range(2):
                away = jnp.where(away >= block_count, away - block_count, away)
            live = (away <= 2) | (key_ids == glob_in[0]) | (key_ids == glob_in[1])
            for k in range(slots):
                live = live | (key_float == ids[b * slots + k:b * slots + k + 1])
            bias = jnp.where(live, 0.0, -jnp.inf).astype(jnp.float32)
            for block in range(block_count):
                bias_buf[b * block_count + block] = jnp.broadcast_to(bias[block:block + 1], (8, lanes))

        def key_rows(which, c):
            lane, zz = c * chunk // lane_keys, c * chunk % lane_keys // shard_tokens
            return kv_buf[h, lane, zz:zz + 2, which].reshape(chunk, width)

        def columns(r):
            return slice(r * tile, (r + 1) * tile)

        def keys_at(c):
            return slice(c * chunk, (c + 1) * chunk)

        def turned_rows(ref, r):
            return ref[h, r * tile_tokens:(r + 1) * tile_tokens].reshape(tile, width).T

        def put_rows(ref, r, turned):
            block = turned.T.reshape(tile_tokens, group, width)
            ref[r * tile_tokens:(r + 1) * tile_tokens, pl.ds(pl.multiple_of(h * group, group), group), :] = block

        tops, totals, deltas = {}, {}, {}

        def turn_keys(which, ref):
            for c in range(chunks):
                ref[:, keys_at(c)] = key_rows(which, c).T

        def scores(r):
            qt = turned_rows(q_buf, r)
            qt_buf[:, columns(r)] = qt
            b = r * tile // (rows // here)
            top = None
            for c in range(chunks):
                lane, zz = c * chunk // lane_keys, c * chunk % lane_keys // shard_tokens
                s = dot(key_rows(0, c), qt)
                for j in range(chunk // BLK):
                    block = ((zz + j // here) * 2 + lane) * here + j % here
                    bias = bias_buf[b * block_count + block]
                    bias = jnp.concatenate([bias] * (tile // lanes), axis=1)
                    piece = s[j * BLK:(j + 1) * BLK].reshape(BLK // 8, 8, tile) + bias[None]
                    at = c * chunk + j * BLK
                    s_buf[at:at + BLK, columns(r)] = piece.reshape(BLK, tile)
                    high = jnp.max(piece, axis=0)
                    top = high if top is None else jnp.maximum(top, high)
            tops[r] = jnp.max(top, axis=0, keepdims=True) * to_log2

        def weights(r):
            total = jnp.zeros((8, tile), jnp.float32)
            for c in range(chunks):
                e = jnp.exp2(s_buf[keys_at(c), columns(r)] * to_log2 - tops[r])
                total = total + jnp.sum(e.reshape(chunk // 8, 8, tile), axis=0)
                e_buf[keys_at(c), columns(r)] = e.astype(jnp.bfloat16)
            totals[r] = jnp.sum(total, axis=0, keepdims=True)

        def outputs(r):
            out_t = dot(vt_buf[...], e_buf[:, columns(r)])
            inverse = 1.0 / totals[r]
            out16 = (out_t * inverse).astype(jnp.bfloat16)
            gt = turned_rows(g_buf, r).astype(jnp.float32)
            deltas[r] = jnp.sum(gt * out16.astype(jnp.float32), axis=0, keepdims=True) * inverse
            gt_buf[:, columns(r)] = (gt * inverse).astype(jnp.bfloat16)
            put_rows(out_ref, r, out16)

        def score_grads(r):
            gt = gt_buf[:, columns(r)]
            for c in range(chunks):
                dp = dot(key_rows(1, c), gt)
                e = e_buf[keys_at(c), columns(r)].astype(jnp.float32)
                ds_buf[keys_at(c), columns(r)] = (e * (dp - deltas[r])).astype(jnp.bfloat16)

        def query_grads(r):
            dq_t = dot(kt_buf[...], ds_buf[:, columns(r)]) * factor
            put_rows(dq_ref, r, dq_t.astype(jnp.bfloat16))

        def key_grads(lane, w):
            left, right = ((qt_buf, ds_buf), (gt_buf, e_buf))[w]
            for zz in range(0, chips, 2):
                at = pl.ds(pl.multiple_of(lane * lane_keys + zz * shard_tokens, chunk), chunk)
                grad = dot(left[...], right[at], NT)
                if w == 0:
                    grad = grad * factor
                grad = grad.astype(jnp.bfloat16)
                for j in range(2):
                    part_buf[h, w, lane, zz + j] = grad[:, j * shard_tokens:(j + 1) * shard_tokens]

        turn_keys(1, vt_buf)
        scores(0)
        scores(1)
        weights(0)
        scores(2)
        weights(1)
        outputs(0)
        hooks[0]()
        scores(3)
        weights(2)
        outputs(1)
        turn_keys(0, kt_buf)
        weights(3)
        outputs(2)
        outputs(3)
        hooks[1]()
        key_grads(1 - core, 1)
        score_grads(0)
        score_grads(1)
        pair_move(h, 1).start()
        hooks[2]()
        score_grads(2)
        score_grads(3)
        key_grads(1 - core, 0)
        pair_move(h, 0).start()
        hooks[3]()
        key_grads(core, 1)
        key_grads(core, 0)
        for r in range(tiles):
            query_grads(r)
        hooks[4]()

    def lead(rank, t):
        return jnp.where(rank == 0, heads, jnp.minimum(jnp.where(rank == 1, 3 + 2 * t, 2 + t), heads))

    def start_loads(h):
        load_q(h).start()
        load_g(h).start()

    own_right(0)
    own_left(0)
    for h in range(3):
        own_sib(h)
    for k in range(1, shards):
        send_ids(k).start()
    each_head(start_loads)
    arrive(0, 1)
    over(1, lead(z, 0), own_right)
    over(1, lead(last - z, 0), own_left)
    for distance in range(2, chips):
        arrive(0, distance)
    ends = jnp.logical_or(z == 0, z == last)
    middle = jnp.logical_not(ends)

    @pl.when(middle)
    def _():
        arrive(1, 1)

    for k in range(1, shards):
        got_ids(k).wait_recv()

    def slot(t, carry):
        over(lead(z, t), lead(z, t + 1), own_right)
        over(lead(last - z, t), lead(last - z, t + 1), own_left)

        @pl.when(t + 3 < heads)
        def _():
            own_sib(t + 3)

        send(kv_buf.at[t, 1 - core], kv_buf.at[t, 1 - core], sib_send, sib_recv.at[t], pair).wait_recv()

        def end_arrive(distance):
            @pl.when(ends)
            def _():
                arrive(t + 1, distance)

        def middle_arrive(*events):
            for when, h, distance in events:
                @pl.when(jnp.logical_and(middle, when))
                def _(h=h, distance=distance):
                    arrive(h, distance)

        def caught(rank_lag):
            low = jnp.where(t == heads - 2, 0, t - rank_lag)
            return low, jnp.where(t < heads - 2, low, t - rank_lag + 1)

        def far(w, rank_lag):
            low, high = caught(rank_lag)
            over(low, high, lambda h: reduce(2, h, w))

        def hook0():
            @pl.when(t > 0)
            def _():
                pair_move(t - 1, 0).wait_recv()
                reduce(0, t - 1, 0)
            end_arrive(1)
            middle_arrive((t == 0, 2, 1), (t == 0, 1, 2))

        def hook1():
            reduce(1, t - 1, 1)
            far(0, 2)
            end_arrive(2)
            middle_arrive((t == 1, 4, 1), (t == 3, 7, 1))

        def hook2():
            end_arrive(3)
            middle_arrive((t == 2, 6, 1), (t > 0, t + 2, 2))

        def hook3():
            middle_arrive((t == 0, 3, 1))

        def hook4():
            pair_move(t, 1).wait_recv()
            reduce(0, t, 1)
            reduce(1, t - 1, 0)
            far(1, 1)
            middle_arrive((t == 0, 2, 2), (t == 1, 5, 1))

        compute(t, [hook0, hook1, hook2, hook3, hook4])
        return carry

    lax.fori_loop(0, heads, slot, 0)

    final = heads - 1

    def finish_both(h):
        finish(h, 1)
        finish(h, 0)

    reduce(2, final - 1, 0)
    reduce(1, final, 1)
    reduce(2, final, 1)
    pair_move(final, 0).wait_recv()
    reduce(0, final, 0)
    over(0, 2, finish_both)
    reduce(1, final, 0)
    over(2, 5, finish_both)
    reduce(2, final, 0)
    over(5, heads, finish_both)

    for which, ref in enumerate((dk_ref, dv_ref)):
        turned = jnp.swapaxes(grads_ref[:, which].astype(jnp.float32), 0, 1)
        ref[...] = turned.astype(jnp.bfloat16)

    def drained(region, sem):
        send(region, region, sem, ids_recv.at[0], pair).wait_send()

    drained(ids_out.at[pl.ds(1, shards - 1)], ids_send)
    drained(kv_buf.at[:, 0], sib_send)
    drained(sib_in, pair_send)
    for zz in range(chips):
        @pl.when(z == zz)
        def _(zz=zz):
            if zz < last:
                drained(kv_buf.at[:, 0, pl.ds(0, zz + 1)], fwd_send)
                drained(right_out.at[:, :, pl.ds(0, last - zz)], right_send)
            if zz > 0:
                drained(kv_buf.at[:, 0, pl.ds(0, chips - zz)], back_send)
                drained(left_out.at[:, :, pl.ds(0, zz)], left_send)


def fused(queries, out_grad, keys, values, rand_blocks, global_blocks, shards):
    tokens, heads, width = queries.shape
    kv_heads = keys.shape[1]
    group = heads // kv_heads
    chips = shards // 2
    rows = tokens * group
    length = tokens * shards
    blocks = length // BLK
    here = tokens // BLK
    bf16, f32 = jnp.bfloat16, jnp.float32
    vmem = pl.BlockSpec(memory_space=pltpu.VMEM)
    smem = pl.BlockSpec(memory_space=pltpu.SMEM)
    anywhere = pl.BlockSpec(memory_space=pl.ANY)
    dma = pltpu.SemaphoreType.DMA
    piece = (2, tokens, width)
    block = pltpu.VMEM((kv_heads, tokens, group, width), bf16)
    hop = pltpu.VMEM((kv_heads, 2, chips, width, tokens), bf16)
    results = pl.pallas_call(
        fused_kernel,
        in_specs=[vmem, smem, vmem, vmem, anywhere, anywhere],
        out_specs=[vmem] * 4,
        out_shape=[
            pltpu.VMEM(queries.shape, bf16),
            pltpu.VMEM(queries.shape, bf16),
            pltpu.VMEM(keys.shape, bf16),
            pltpu.VMEM(keys.shape, bf16),
        ],
        scratch_shapes=[pltpu.VMEM((kv_heads,) + piece, bf16)] + [block] * 2
        + [
            pltpu.VMEM((kv_heads, 2, chips) + piece, bf16),
            pltpu.VMEM((kv_heads, 2, 2, chips, width, tokens), bf16),
        ]
        + [hop] * 5
        + [
            pltpu.VMEM((shards, 8, 128), f32),
            pltpu.VMEM((shards, 8, 128), f32),
            pltpu.VMEM((here * blocks, 8, 128), f32),
            pltpu.VMEM((length, rows), f32),
            pltpu.VMEM((length, rows), bf16),
            pltpu.VMEM((length, rows), bf16),
            pltpu.VMEM((width, length), bf16),
            pltpu.VMEM((width, length), bf16),
            pltpu.VMEM((width, rows), bf16),
            pltpu.VMEM((width, rows), bf16),
        ]
        + [dma((kv_heads,))] * 2
        + [dma] * 7
        + [dma((shards,)), dma((kv_heads,)), dma((kv_heads, chips)), dma((kv_heads, 2))]
        + [dma((kv_heads, 2, chips))] * 2,
        compiler_params=pltpu.CompilerParams(
            collective_id=0, has_side_effects=True, vmem_limit_bytes=50 * 1024 * 1024
        ),
        name="fused",
    )(rand_blocks.transpose(2, 0, 1), global_blocks, keys, values, queries, out_grad)
    return results


def body(shards, queries, keys, values, out_grad, rand_blocks, global_blocks):
    tokens, kv_heads, width = keys.shape
    here = tokens // BLK
    block_count = rand_blocks.shape[1]
    group = queries.shape[1] // kv_heads
    me = lax.axis_index("ctx")
    if (shards == kv_heads == group == 8 and here == 2 and rand_blocks.shape[2] == 3
            and global_blocks.shape[0] == 2):
        return fused(queries, out_grad, keys, values, rand_blocks, global_blocks, shards)
    kv_here = jnp.stack([keys.transpose(1, 0, 2), values.transpose(1, 0, 2)], axis=1)
    kv = lax.all_gather(kv_here, "ctx", axis=0)
    rand_all = lax.all_gather(rand_blocks, "ctx", axis=0, tiled=True)
    bias = row_bias(rand_all, global_blocks, me * here, here, block_count, kv_heads)
    output, query_grad, parts = local_attention(queries, out_grad, kv, bias)
    sums = lax.psum_scatter(parts, "ctx", scatter_dimension=0, tiled=False)
    grads = sums.transpose(1, 2, 0, 3)
    return output, query_grad, grads[0], grads[1]


def solution(mesh):
    split = P(("dp", "ctx"), None, None)
    return jax.shard_map(
        functools.partial(body, mesh.shape["ctx"]),
        mesh=mesh,
        in_specs=(split, split, split, split, split, P("dp")),
        out_specs=(split, split, split, split),
        check_vma=False,
    )
```

```python
import functools
import math

import jax
import jax.numpy as jnp
from jax import lax
from jax.experimental import pallas as pl
from jax.experimental.pallas import tpu as pltpu
from jax.sharding import PartitionSpec as P

BLK = 64
NT = (((1,), (1,)), ((), ()))
NN = (((1,), (0,)), ((), ()))
HIDDEN = -1e30


def dot(left, right, dims=NN):
    return lax.dot_general(left, right, dims, preferred_element_type=jnp.float32)


def flat_rows(block):
    rows = block.shape[0] * block.shape[1]
    return block.astype(jnp.float32).reshape(rows, block.shape[2])


def for_chunks(count, step, init):
    return lax.fori_loop(0, count, step, init, unroll=count <= 4)


def attention(geometry, q_ref, g_ref, kv_ref, bias_ref, out_ref, dq_ref, dkv_ref, s_buf, e_buf, acc):
    chunk, row_tile = geometry
    shards, _, _, shard_tokens, width = kv_ref.shape
    length = shards * shard_tokens
    count = length // chunk
    tokens, group, _ = q_ref.shape
    rows = tokens * group
    tiles = rows // row_tile
    tile_tokens = row_tile // group
    factor = 1.0 / math.sqrt(width)
    to_log2 = factor * math.log2(math.e)
    per_chunk = chunk // shard_tokens

    def kv_chunk(which, c):
        return kv_ref[pl.ds(c * per_chunk, per_chunk), 0, which].reshape(chunk, width)

    for tile in range(tiles):
        t0 = tile * tile_tokens
        lanes = pl.ds(tile * row_tile, row_tile)
        q = flat_rows(q_ref[pl.ds(t0, tile_tokens)]).astype(jnp.bfloat16)
        g32 = flat_rows(g_ref[pl.ds(t0, tile_tokens)])

        def score_step(c, top):
            s = dot(kv_chunk(0, c), q, NT) * to_log2
            blocks = chunk // BLK
            bias = bias_ref[0, pl.ds(c * blocks, blocks), :, lanes]
            s = (s.reshape(blocks, BLK, row_tile) + bias).reshape(chunk, row_tile)
            s_buf[pl.ds(c * chunk, chunk)] = s
            return jnp.maximum(top, jnp.max(s, axis=0, keepdims=True))

        top = for_chunks(count, score_step, jnp.full((1, row_tile), -jnp.inf, jnp.float32))

        def weight_step(c, carry):
            total, out_t = carry
            e = jnp.exp2(s_buf[pl.ds(c * chunk, chunk)] - top)
            total = total + jnp.sum(e, axis=0, keepdims=True)
            e16 = e.astype(jnp.bfloat16)
            e_buf[pl.ds(c * chunk, chunk)] = e16
            out_t = out_t + dot(kv_chunk(1, c).T, e16)
            return total, out_t

        total, out_t = for_chunks(
            count,
            weight_step,
            (jnp.zeros((1, row_tile), jnp.float32), jnp.zeros((width, row_tile), jnp.float32)),
        )
        inverse = 1.0 / total
        out16 = (out_t * inverse).T.astype(jnp.bfloat16)
        out32 = out16.astype(jnp.float32)
        out_ref[pl.ds(t0, tile_tokens)] = out32.reshape(tile_tokens, group, width).astype(jnp.bfloat16)
        delta = jnp.sum((g32 * out32).T, axis=0, keepdims=True) * inverse
        g16 = (g32.T * inverse).T.astype(jnp.bfloat16)

        def grad_step(c, dq_t):
            at = pl.ds(c * chunk, chunk)
            e16 = e_buf[at]
            dp = dot(kv_chunk(1, c), g16, NT)
            ds = (e16.astype(jnp.float32) * (dp - delta)).astype(jnp.bfloat16)
            dk = dot(ds, q)
            dv = dot(e16, g16)
            if tile > 0:
                dk = dk + acc[0, at]
                dv = dv + acc[1, at]
            if tile < tiles - 1:
                acc[0, at] = dk
                acc[1, at] = dv
            else:
                shape = (per_chunk, shard_tokens, width)
                spot = pl.ds(c * per_chunk, per_chunk)
                dkv_ref[spot, 0, 0] = (dk * factor).astype(jnp.bfloat16).reshape(shape)
                dkv_ref[spot, 0, 1] = dv.astype(jnp.bfloat16).reshape(shape)
            return dq_t + dot(kv_chunk(0, c).T, ds)

        dq_t = for_chunks(count, grad_step, jnp.zeros((width, row_tile), jnp.float32))
        dq = (dq_t * factor).T.reshape(tile_tokens, group, width)
        dq_ref[pl.ds(t0, tile_tokens)] = dq.astype(jnp.bfloat16)


def local_attention(queries, out_grad, kv, bias):
    tokens, heads, width = queries.shape
    shards, kv_heads, _, shard_tokens, _ = kv.shape
    group = heads // kv_heads
    length = shards * shard_tokens
    rows = tokens * group
    chunk = math.gcd(length, 256)
    row_tile = rows
    while row_tile * length > (1 << 21) and row_tile > 128:
        row_tile //= 2
    acc_rows = length if row_tile < rows else 8
    blocks = length // BLK
    q_spec = pl.BlockSpec((tokens, group, width), lambda g: (0, g, 0))
    kv_spec = pl.BlockSpec((shards, 1, 2, shard_tokens, width), lambda g: (0, g, 0, 0, 0))
    return pl.pallas_call(
        functools.partial(attention, (chunk, row_tile)),
        grid=(kv_heads,),
        in_specs=[
            q_spec,
            q_spec,
            kv_spec,
            pl.BlockSpec((1, blocks, 1, rows), lambda g: (g, 0, 0, 0)),
        ],
        out_specs=[q_spec, q_spec, kv_spec],
        out_shape=[
            jax.ShapeDtypeStruct(queries.shape, jnp.bfloat16),
            jax.ShapeDtypeStruct(queries.shape, jnp.bfloat16),
            jax.ShapeDtypeStruct(kv.shape, jnp.bfloat16),
        ],
        scratch_shapes=[
            pltpu.VMEM((length, row_tile), jnp.float32),
            pltpu.VMEM((length, row_tile), jnp.bfloat16),
            pltpu.VMEM((2, acc_rows, width), jnp.float32),
        ],
        compiler_params=pltpu.CompilerParams(vmem_limit_bytes=60 * 1024 * 1024),
        name="attention",
    )(queries, out_grad, kv, bias)


def row_bias(rand_all, global_blocks, first, here, block_count, kv_heads):
    heads = rand_all.shape[0]
    group = heads // kv_heads
    mine = lax.dynamic_slice_in_dim(rand_all, first, here, axis=1)
    ids = first + jnp.arange(here, dtype=jnp.int32)
    key_ids = jnp.arange(block_count, dtype=jnp.int32)
    away = (key_ids[None, :] - ids[:, None] + block_count + 1) % block_count
    common = (away <= 2) | jnp.any(key_ids[None, :, None] == global_blocks[None, None, :], axis=2)
    chosen = jnp.any(mine[:, :, None, :] == key_ids[None, None, :, None], axis=3)
    live = chosen | common[None]
    bias = jnp.where(live, 0.0, -jnp.inf).astype(jnp.float32)
    bias = bias.reshape(kv_heads, group, here, block_count).transpose(0, 3, 2, 1)
    bias = jnp.broadcast_to(bias[:, :, :, None, :], (kv_heads, block_count, here, BLK, group))
    return bias.reshape(kv_heads, block_count, 1, here * BLK * group)


def fused_kernel(
    rand_in, glob_in, k_in, v_in, q_hbm, g_hbm, out_ref, dq_ref, dk_ref, dv_ref,
    grads_ref, q_buf, g_buf, kv_buf, part_buf, sib_in, right_in, left_in, right_out, left_out,
    ids_out, ids_buf, mark_buf, e_buf, ds_buf, vt_buf, kt_buf, qt_buf, gt_buf,
    q_sem, g_sem,
    ids_send, sib_send, fwd_send, back_send, far_send, pair_send, right_send, left_send,
    ids_recv, sib_recv, kv_recv, pair_recv, right_recv, left_recv,
):
    heads, _, chips, _, shard_tokens, width = kv_buf.shape
    shards = 2 * chips
    _, tokens, group, _ = q_buf.shape
    rows = tokens * group
    here = tokens // BLK
    block_count = shards * here
    lane_keys = chips * shard_tokens
    tile = 256
    tiles = rows // tile
    tile_tokens = tile // group
    chunk = 2 * shard_tokens
    chunks = shards * shard_tokens // chunk
    factor = 1.0 / math.sqrt(width)
    to_log2 = factor * math.log2(math.e)
    me = lax.axis_index("ctx")
    z, core = me // 2, me % 2
    pair = z * 2 + 1 - core
    ahead, behind = me + 2, me - 2
    last = chips - 1

    barrier = pltpu.get_barrier_semaphore()
    for k in range(1, shards):
        pl.semaphore_signal(
            barrier, inc=1, device_id={"ctx": lax.rem(me + k, shards)}, device_id_type=pl.DeviceIdType.MESH
        )

    def send(source, target, send_sem, recv_sem, to):
        return pltpu.make_async_remote_copy(
            src_ref=source, dst_ref=target, send_sem=send_sem, recv_sem=recv_sem,
            device_id={"ctx": to}, device_id_type=pl.DeviceIdType.MESH,
        )

    def send_ids(k):
        to = lax.rem(me + k, shards)
        return send(ids_out.at[to], ids_buf.at[me], ids_send, ids_recv.at[me], to)

    def got_ids(k):
        origin = lax.rem(me + k, shards)
        return send(ids_out.at[origin], ids_buf.at[origin], ids_send, ids_recv.at[origin], origin)

    def kv_move(h, origin, send_sem, to):
        spot = kv_buf.at[h, core, origin]
        return send(spot, spot, send_sem, kv_recv.at[h, origin], to)

    def right_kv(h, origin):
        return kv_move(h, origin, fwd_send, ahead)

    def left_kv(h, origin):
        return kv_move(h, origin, back_send, behind)

    def sib_kv(h, origin):
        spot = kv_buf.at[h, core, origin]
        return send(spot, spot, sib_send, sib_recv.at[h], pair)

    def pair_move(h, w):
        return send(part_buf.at[h, w, 1 - core], sib_in.at[h, w], pair_send, pair_recv.at[h, w], pair)

    def side_move(side, h, zd, w=None):
        out, arrived = (right_out, right_in) if side == 0 else (left_out, left_in)
        sems = (right_send, right_recv) if side == 0 else (left_send, left_recv)
        at, slot = (h, zd), h
        if w is not None:
            at, slot = (h, zd, w), h + w
        return send(out.at[at], arrived.at[at], sems[0], sems[1].at[slot, zd], ahead if side == 0 else behind)

    def head_columns(ref, h):
        return ref.at[:, pl.ds(pl.multiple_of(h * group, group), group), :]

    def load_q(h):
        return pltpu.make_async_copy(head_columns(q_hbm, h), q_buf.at[h], q_sem.at[h])

    def load_g(h):
        return pltpu.make_async_copy(head_columns(g_hbm, h), g_buf.at[h], g_sem.at[h])

    def each_head(step):
        def run(h, carry):
            step(h)
            return carry
        lax.fori_loop(0, heads, run, 0)

    for which, ref in enumerate((k_in, v_in)):
        turned = jnp.swapaxes(ref[...].astype(jnp.float32), 0, 1)
        kv_buf[:, core, z, which] = turned.astype(jnp.bfloat16)

    slots = rand_in.shape[0]
    lanes = ids_buf.shape[2]
    spread = lax.broadcasted_iota(jnp.int32, (group, lanes), 1) % group
    spread = (spread == lax.broadcasted_iota(jnp.int32, (group, lanes), 0)).astype(jnp.float32)
    for k in range(slots):
        picks = lax.dot_general(
            rand_in[k].astype(jnp.float32), spread, (((0,), (0,)), ((), ())), preferred_element_type=jnp.float32
        )
        for to in range(shards):
            for b in range(here):
                spot = to * here + b
                ids_out[to, b * slots + k:b * slots + k + 1] = picks[spot:spot + 1]
    ids_buf[me] = ids_out[me]

    length = shards * shard_tokens
    spot = lax.broadcasted_iota(jnp.int32, (length, width), 0)
    spot_lane, spot_chip = spot // lane_keys, spot % lane_keys // shard_tokens
    spot_block = (spot_chip * 2 + spot_lane) * here + spot % shard_tokens // BLK
    column = lax.broadcasted_iota(jnp.int32, (length, width), 1)
    ones = jnp.logical_and(column >= block_count, column < block_count + 3)
    mark_buf[...] = jnp.logical_or(column == spot_block, ones).astype(jnp.float32).astype(jnp.bfloat16)
    vt_buf[width:, :] = jnp.ones((16, length), jnp.bfloat16)
    qt_buf[width:, :] = jnp.zeros((width, rows), jnp.bfloat16)
    gt_buf[width:, :] = jnp.zeros((width, rows), jnp.bfloat16)

    pl.semaphore_wait(barrier, shards - 1)

    def own_right(h):
        @pl.when(z < last)
        def _():
            right_kv(h, z).start()

    def own_left(h):
        @pl.when(z > 0)
        def _():
            left_kv(h, z).start()

    def own_sib(h):
        sib_kv(h, z).start()

    ends = jnp.logical_or(z == 0, z == last)
    middle = jnp.logical_not(ends)

    def landed(h, origin):
        kv_move(h, origin, fwd_send, pair).wait_recv()

    def end_arrive(h, distance):
        origin = jnp.where(z == 0, distance, last - distance)
        landed(h, origin)
        sib_kv(h, origin).start()

    def near_arrive(h):
        landed(h, z - 1)
        right_kv(h, z - 1).start()
        sib_kv(h, z - 1).start()
        landed(h, z + 1)
        left_kv(h, z + 1).start()
        sib_kv(h, z + 1).start()

    def far_origin():
        return jnp.where(z == 1, last, 0)

    def far_arrive(h):
        origin = far_origin()
        landed(h, origin)
        kv_move(h, origin, far_send, jnp.where(z == 1, behind, ahead)).start()
        sib_kv(h, origin).start()

    def over(low, high, step):
        def run(h, carry):
            step(h)
            return carry
        lax.fori_loop(low, high, run, 0)

    def combined(h, zd, w=None):
        at = slice(None) if w is None else w
        return part_buf[h, at, core, zd].astype(jnp.float32) + sib_in[h, at, zd].astype(jnp.float32)

    def reduce(rank, h, w=None, only=None):
        for side in range(2):
            zz = rank if side == 0 else last - rank
            targets = list(range(last, zz, -1) if side == 0 else range(zz))
            if only is not None:
                targets = targets[only:only + 1]
            out, arrived = (right_out, right_in) if side == 0 else (left_out, left_in)

            @pl.when(z == zz)
            def _(side=side, targets=targets, out=out, arrived=arrived):
                for zd in targets:
                    at = (h, zd) if w is None else (h, zd, w)
                    total = combined(h, zd, w)
                    if rank > 0:
                        side_move(side, h, zd, w).wait_recv()
                        total = total + arrived[at].astype(jnp.float32)
                    out[at] = total.astype(jnp.bfloat16)
                    side_move(side, h, zd, w).start()

    def finish(h, w=None):
        for zz in range(chips):
            @pl.when(z == zz)
            def _(zz=zz):
                at = (h, zz) if w is None else (h, zz, w)
                total = combined(h, zz, w)
                if zz > 0:
                    side_move(0, h, zz, w).wait_recv()
                    total = total + right_in[at].astype(jnp.float32)
                if zz < last:
                    side_move(1, h, zz, w).wait_recv()
                    total = total + left_in[at].astype(jnp.float32)
                for which in range(2) if w is None else (w,):
                    piece = total[which] if w is None else total
                    grads_ref[h, which] = piece.T.astype(jnp.bfloat16)

    def compute(h, hooks):
        load_q(h).wait()
        load_g(h).wait()
        ids = ids_buf[h]
        key_ids = lax.broadcasted_iota(jnp.int32, (block_count, lanes), 0)
        key_float = key_ids.astype(jnp.float32)
        for b in range(here):
            away = key_ids - (me * here + b) + (block_count + 1)
            for _ in range(2):
                away = jnp.where(away >= block_count, away - block_count, away)
            live = (away <= 2) | (key_ids == glob_in[0]) | (key_ids == glob_in[1])
            for k in range(slots):
                live = live | (key_float == ids[b * slots + k:b * slots + k + 1])
            bias = jnp.where(live, 0.0, HIDDEN).astype(jnp.float32).astype(jnp.bfloat16)
            half = rows // here
            qt_buf[width:width + block_count, b * half:(b + 1) * half] = jnp.concatenate([bias] * (half // lanes), axis=1)

        def key_rows(which, c):
            lane, zz = c * chunk // lane_keys, c * chunk % lane_keys // shard_tokens
            return kv_buf[h, lane, zz:zz + 2, which].reshape(chunk, width)

        def columns(r):
            return slice(r * tile, (r + 1) * tile)

        def keys_at(c):
            return slice(c * chunk, (c + 1) * chunk)

        def turned_rows(ref, r):
            return ref[h, r * tile_tokens:(r + 1) * tile_tokens].reshape(tile, width).T

        def put_rows(ref, r, turned):
            block = turned.T.reshape(tile_tokens, group, width)
            ref[r * tile_tokens:(r + 1) * tile_tokens, pl.ds(pl.multiple_of(h * group, group), group), :] = block

        tops = {}

        def turn_keys(which, ref):
            for c in range(chunks):
                ref[:width, keys_at(c)] = key_rows(which, c).T

        def marked(which, at):
            spot = at.start
            keys = kv_buf[h, spot // lane_keys, spot % lane_keys // shard_tokens, which, pl.ds(spot % shard_tokens, 128)]
            return jnp.concatenate([keys, mark_buf[at]], axis=1)

        def slabs(size):
            return [slice(at, at + size) for at in range(0, length, size)]

        def scores(r):
            qt_buf[:width, columns(r)] = turned_rows(q_buf, r)
            right = qt_buf[:, columns(r)]
            top = None
            for at in slabs(128):
                s = dot(marked(0, at), right)
                high = jnp.max(s.reshape(128 // 8, 8, tile), axis=0)
                top = high if top is None else jnp.maximum(top, high)
            tops[r] = jnp.max(top, axis=0, keepdims=True) * to_log2

        def weights(r):
            right = qt_buf[:, columns(r)]
            for at in slabs(128):
                e = jnp.exp2(dot(marked(0, at), right) * to_log2 - tops[r])
                e_buf[at, columns(r)] = e.astype(jnp.bfloat16)

        def outputs(r):
            out_t = dot(vt_buf[...], e_buf[:, columns(r)])
            inverse = 1.0 / out_t[width:width + 1]
            out16 = (out_t[:width] * inverse).astype(jnp.bfloat16)
            gt = turned_rows(g_buf, r).astype(jnp.float32)
            rest = jnp.sum(gt * out16.astype(jnp.float32), axis=0, keepdims=True) * -inverse
            gt_buf[:width, columns(r)] = (gt * inverse).astype(jnp.bfloat16)
            level = lax.broadcasted_iota(jnp.int32, (16, tile), 0)
            split = jnp.zeros((16, tile), jnp.float32)
            for k in range(3):
                part = rest.astype(jnp.bfloat16).astype(jnp.float32)
                split = jnp.where(level == k, part, split)
                rest = rest - part
            gt_buf[width + block_count:width + block_count + 16, columns(r)] = split.astype(jnp.bfloat16)
            put_rows(out_ref, r, out16)

        def score_grads(r):
            right = gt_buf[:, columns(r)]
            for at in slabs(128):
                dp = dot(marked(1, at), right).astype(jnp.bfloat16)
                ds_buf[at, columns(r)] = e_buf[at, columns(r)] * dp

        def query_grads(r):
            dq_t = dot(kt_buf[...], ds_buf[:, columns(r)]) * factor
            put_rows(dq_ref, r, dq_t.astype(jnp.bfloat16))

        def key_grads(lane, w):
            left, right = ((qt_buf, ds_buf), (gt_buf, e_buf))[w]
            for zz in range(0, chips, 2):
                at = pl.ds(pl.multiple_of(lane * lane_keys + zz * shard_tokens, chunk), chunk)
                grad = dot(left[:width], right[at], NT)
                if w == 0:
                    grad = grad * factor
                grad = grad.astype(jnp.bfloat16)
                for j in range(2):
                    part_buf[h, w, lane, zz + j] = grad[:, j * shard_tokens:(j + 1) * shard_tokens]

        turn_keys(1, vt_buf)
        scores(0)
        scores(1)
        weights(0)
        scores(2)
        weights(1)
        outputs(0)
        scores(3)
        weights(2)
        outputs(1)
        turn_keys(0, kt_buf)
        weights(3)
        outputs(2)
        outputs(3)
        hooks[0]()
        key_grads(1 - core, 1)
        pair_move(h, 1).start()
        for r in range(tiles):
            score_grads(r)
        key_grads(1 - core, 0)
        pair_move(h, 0).start()
        key_grads(core, 1)
        key_grads(core, 0)
        for r in range(tiles):
            query_grads(r)

    def lead(rank, t):
        return jnp.where(rank == 0, heads, jnp.minimum(jnp.where(rank == 1, 3 + 2 * t, 2 + t), heads))

    def start_loads(h):
        load_q(h).start()
        load_g(h).start()

    own_right(0)
    own_left(0)
    for h in range(3):
        own_sib(h)
    for k in range(1, shards):
        send_ids(k).start()
    each_head(start_loads)

    @pl.when(middle)
    def _():
        near_arrive(0)

    @pl.when(ends)
    def _():
        end_arrive(0, 1)
    over(1, lead(z, 0), own_right)
    over(1, lead(last - z, 0), own_left)

    @pl.when(middle)
    def _():
        far_arrive(0)
        near_arrive(1)

    @pl.when(ends)
    def _():
        end_arrive(0, 2)
        end_arrive(0, 3)

    for k in range(1, shards):
        got_ids(k).wait_recv()

    final = heads - 1

    def near_done(t):
        return jnp.minimum(jnp.minimum(2 + 2 * t, 4 + t), heads)

    def slot(t, carry):
        over(lead(z, t), lead(z, t + 1), own_right)
        over(lead(last - z, t), lead(last - z, t + 1), own_left)

        @pl.when(t + 3 < heads)
        def _():
            own_sib(t + 3)

        @pl.when(jnp.logical_and(middle, t == 1))
        def _():
            far_arrive(2)

        send(kv_buf.at[t, 1 - core], kv_buf.at[t, 1 - core], sib_send, sib_recv.at[t], pair).wait_recv()

        def hook():
            @pl.when(t > 0)
            def _():
                pair_move(t - 1, 1).wait_recv()
                pair_move(t - 1, 0).wait_recv()
                reduce(0, t - 1)

            @pl.when(t > 1)
            def _():
                reduce(1, t - 2)

            low = jnp.where(t == final - 1, 0, t - 3)
            over(low, jnp.where(t < final - 1, low, t - 2), lambda h: reduce(2, h))

            @pl.when(jnp.logical_and(ends, t < final))
            def _():
                for distance in range(1, chips):
                    end_arrive(t + 1, distance)

            @pl.when(middle)
            def _():
                over(near_done(t), near_done(t + 1), near_arrive)
                far = jnp.where(t == 0, 1, t + 2)
                over(far, jnp.minimum(far + 1, heads), far_arrive)

        compute(t, [hook])
        return carry

    lax.fori_loop(0, heads, slot, 0)

    reduce(1, final - 1)
    reduce(2, final - 2)
    reduce(2, final - 1)
    pair_move(final, 1).wait_recv()
    reduce(0, final, 1, 0)
    pair_move(final, 0).wait_recv()
    for rank, w, only in ((0, 0, 0), (0, 1, 1), (0, 0, 1), (0, 1, 2), (0, 0, 2),
                          (1, 1, 0), (1, 0, 0), (2, 1, 0), (1, 1, 1), (2, 0, 0), (1, 0, 1)):
        reduce(rank, final, w, only)
    over(0, final, finish)
    finish(final, 1)
    finish(final, 0)

    for which, ref in enumerate((dk_ref, dv_ref)):
        turned = jnp.swapaxes(grads_ref[:, which].astype(jnp.float32), 0, 1)
        ref[...] = turned.astype(jnp.bfloat16)

    def drained(region, sem):
        send(region, region, sem, ids_recv.at[0], pair).wait_send()

    drained(ids_out.at[pl.ds(1, shards - 1)], ids_send)
    drained(kv_buf.at[:, 0], sib_send)
    drained(sib_in, pair_send)
    @pl.when(middle)
    def _():
        drained(kv_buf.at[:, 0, pl.ds(0, 2)], fwd_send)
        drained(kv_buf.at[:, 0, pl.ds(0, 2)], back_send)
        drained(kv_buf.at[:, 0, 0], far_send)

    for zz in range(chips):
        @pl.when(z == zz)
        def _(zz=zz):
            if zz == 0:
                drained(kv_buf.at[:, 0, 0], fwd_send)
            if zz == last:
                drained(kv_buf.at[:, 0, 0], back_send)
            if zz < last:
                drained(right_out.at[:, pl.ds(0, last - zz)], right_send)
            if zz > 0:
                drained(left_out.at[:, pl.ds(0, zz)], left_send)


def fused(queries, out_grad, keys, values, rand_blocks, global_blocks, shards):
    tokens, heads, width = queries.shape
    kv_heads = keys.shape[1]
    group = heads // kv_heads
    chips = shards // 2
    rows = tokens * group
    length = tokens * shards
    blocks = length // BLK
    here = tokens // BLK
    bf16, f32 = jnp.bfloat16, jnp.float32
    vmem = pl.BlockSpec(memory_space=pltpu.VMEM)
    smem = pl.BlockSpec(memory_space=pltpu.SMEM)
    anywhere = pl.BlockSpec(memory_space=pl.ANY)
    dma = pltpu.SemaphoreType.DMA
    piece = (2, tokens, width)
    block = pltpu.VMEM((kv_heads, tokens, group, width), bf16)
    hop = pltpu.VMEM((kv_heads, chips, 2, width, tokens), bf16)
    gift = pltpu.VMEM((kv_heads, 2, chips, width, tokens), bf16)
    results = pl.pallas_call(
        fused_kernel,
        in_specs=[vmem, smem, vmem, vmem, anywhere, anywhere],
        out_specs=[vmem] * 4,
        out_shape=[
            pltpu.VMEM(queries.shape, bf16),
            pltpu.VMEM(queries.shape, bf16),
            pltpu.VMEM(keys.shape, bf16),
            pltpu.VMEM(keys.shape, bf16),
        ],
        scratch_shapes=[pltpu.VMEM((kv_heads,) + piece, bf16)] + [block] * 2
        + [
            pltpu.VMEM((kv_heads, 2, chips) + piece, bf16),
            pltpu.VMEM((kv_heads, 2, 2, chips, width, tokens), bf16),
        ]
        + [gift]
        + [hop] * 4
        + [
            pltpu.VMEM((shards, 8, 128), f32),
            pltpu.VMEM((shards, 8, 128), f32),
            pltpu.VMEM((length, 128), bf16),
            pltpu.VMEM((length, rows), bf16),
            pltpu.VMEM((length, rows), bf16),
            pltpu.VMEM((width + 16, length), bf16),
            pltpu.VMEM((width, length), bf16),
            pltpu.VMEM((2 * width, rows), bf16),
            pltpu.VMEM((2 * width, rows), bf16),
        ]
        + [dma((kv_heads,))] * 2
        + [dma] * 8
        + [dma((shards,)), dma((kv_heads,)), dma((kv_heads, chips)), dma((kv_heads, 2))]
        + [dma((kv_heads + 1, chips))] * 2,
        compiler_params=pltpu.CompilerParams(
            collective_id=0, has_side_effects=True, vmem_limit_bytes=50 * 1024 * 1024
        ),
        name="fused",
    )(rand_blocks.transpose(2, 0, 1), global_blocks, keys, values, queries, out_grad)
    return results


def body(shards, queries, keys, values, out_grad, rand_blocks, global_blocks):
    tokens, kv_heads, width = keys.shape
    here = tokens // BLK
    block_count = rand_blocks.shape[1]
    group = queries.shape[1] // kv_heads
    me = lax.axis_index("ctx")
    if (shards == kv_heads == group == 8 and here == 2 and rand_blocks.shape[2] == 3
            and global_blocks.shape[0] == 2):
        return fused(queries, out_grad, keys, values, rand_blocks, global_blocks, shards)
    kv_here = jnp.stack([keys.transpose(1, 0, 2), values.transpose(1, 0, 2)], axis=1)
    kv = lax.all_gather(kv_here, "ctx", axis=0)
    rand_all = lax.all_gather(rand_blocks, "ctx", axis=0, tiled=True)
    bias = row_bias(rand_all, global_blocks, me * here, here, block_count, kv_heads)
    output, query_grad, parts = local_attention(queries, out_grad, kv, bias)
    sums = lax.psum_scatter(parts, "ctx", scatter_dimension=0, tiled=False)
    grads = sums.transpose(1, 2, 0, 3)
    return output, query_grad, grads[0], grads[1]


def solution(mesh):
    split = P(("dp", "ctx"), None, None)
    return jax.shard_map(
        functools.partial(body, mesh.shape["ctx"]),
        mesh=mesh,
        in_specs=(split, split, split, split, split, P("dp")),
        out_specs=(split, split, split, split),
        check_vma=False,
    )
```

```python
import functools
import math

import jax
import jax.numpy as jnp
from jax import lax
from jax.experimental import pallas as pl
from jax.experimental.pallas import tpu as pltpu
from jax.sharding import PartitionSpec as P

BLK = 64
NT = (((1,), (1,)), ((), ()))
NN = (((1,), (0,)), ((), ()))
HIDDEN = -1e30
COARSE = jnp.float8_e4m3fn
COARSE_MAX = 448.0


def dot(left, right, dims=NN):
    return lax.dot_general(left, right, dims, preferred_element_type=jnp.float32)


def flat_rows(block):
    rows = block.shape[0] * block.shape[1]
    return block.astype(jnp.float32).reshape(rows, block.shape[2])


def for_chunks(count, step, init):
    return lax.fori_loop(0, count, step, init, unroll=count <= 4)


def attention(geometry, q_ref, g_ref, kv_ref, bias_ref, out_ref, dq_ref, dkv_ref, s_buf, e_buf, acc):
    chunk, row_tile = geometry
    shards, _, _, shard_tokens, width = kv_ref.shape
    length = shards * shard_tokens
    count = length // chunk
    tokens, group, _ = q_ref.shape
    rows = tokens * group
    tiles = rows // row_tile
    tile_tokens = row_tile // group
    factor = 1.0 / math.sqrt(width)
    to_log2 = factor * math.log2(math.e)
    per_chunk = chunk // shard_tokens

    def kv_chunk(which, c):
        return kv_ref[pl.ds(c * per_chunk, per_chunk), 0, which].reshape(chunk, width)

    for tile in range(tiles):
        t0 = tile * tile_tokens
        lanes = pl.ds(tile * row_tile, row_tile)
        q = flat_rows(q_ref[pl.ds(t0, tile_tokens)]).astype(jnp.bfloat16)
        g32 = flat_rows(g_ref[pl.ds(t0, tile_tokens)])

        def score_step(c, top):
            s = dot(kv_chunk(0, c), q, NT) * to_log2
            blocks = chunk // BLK
            bias = bias_ref[0, pl.ds(c * blocks, blocks), :, lanes]
            s = (s.reshape(blocks, BLK, row_tile) + bias).reshape(chunk, row_tile)
            s_buf[pl.ds(c * chunk, chunk)] = s
            return jnp.maximum(top, jnp.max(s, axis=0, keepdims=True))

        top = for_chunks(count, score_step, jnp.full((1, row_tile), -jnp.inf, jnp.float32))

        def weight_step(c, carry):
            total, out_t = carry
            e = jnp.exp2(s_buf[pl.ds(c * chunk, chunk)] - top)
            total = total + jnp.sum(e, axis=0, keepdims=True)
            e16 = e.astype(jnp.bfloat16)
            e_buf[pl.ds(c * chunk, chunk)] = e16
            out_t = out_t + dot(kv_chunk(1, c).T, e16)
            return total, out_t

        total, out_t = for_chunks(
            count,
            weight_step,
            (jnp.zeros((1, row_tile), jnp.float32), jnp.zeros((width, row_tile), jnp.float32)),
        )
        inverse = 1.0 / total
        out16 = (out_t * inverse).T.astype(jnp.bfloat16)
        out32 = out16.astype(jnp.float32)
        out_ref[pl.ds(t0, tile_tokens)] = out32.reshape(tile_tokens, group, width).astype(jnp.bfloat16)
        delta = jnp.sum((g32 * out32).T, axis=0, keepdims=True) * inverse
        g16 = (g32.T * inverse).T.astype(jnp.bfloat16)

        def grad_step(c, dq_t):
            at = pl.ds(c * chunk, chunk)
            e16 = e_buf[at]
            dp = dot(kv_chunk(1, c), g16, NT)
            ds = (e16.astype(jnp.float32) * (dp - delta)).astype(jnp.bfloat16)
            dk = dot(ds, q)
            dv = dot(e16, g16)
            if tile > 0:
                dk = dk + acc[0, at]
                dv = dv + acc[1, at]
            if tile < tiles - 1:
                acc[0, at] = dk
                acc[1, at] = dv
            else:
                shape = (per_chunk, shard_tokens, width)
                spot = pl.ds(c * per_chunk, per_chunk)
                dkv_ref[spot, 0, 0] = (dk * factor).astype(jnp.bfloat16).reshape(shape)
                dkv_ref[spot, 0, 1] = dv.astype(jnp.bfloat16).reshape(shape)
            return dq_t + dot(kv_chunk(0, c).T, ds)

        dq_t = for_chunks(count, grad_step, jnp.zeros((width, row_tile), jnp.float32))
        dq = (dq_t * factor).T.reshape(tile_tokens, group, width)
        dq_ref[pl.ds(t0, tile_tokens)] = dq.astype(jnp.bfloat16)


def local_attention(queries, out_grad, kv, bias):
    tokens, heads, width = queries.shape
    shards, kv_heads, _, shard_tokens, _ = kv.shape
    group = heads // kv_heads
    length = shards * shard_tokens
    rows = tokens * group
    chunk = math.gcd(length, 256)
    row_tile = rows
    while row_tile * length > (1 << 21) and row_tile > 128:
        row_tile //= 2
    acc_rows = length if row_tile < rows else 8
    blocks = length // BLK
    q_spec = pl.BlockSpec((tokens, group, width), lambda g: (0, g, 0))
    kv_spec = pl.BlockSpec((shards, 1, 2, shard_tokens, width), lambda g: (0, g, 0, 0, 0))
    return pl.pallas_call(
        functools.partial(attention, (chunk, row_tile)),
        grid=(kv_heads,),
        in_specs=[
            q_spec,
            q_spec,
            kv_spec,
            pl.BlockSpec((1, blocks, 1, rows), lambda g: (g, 0, 0, 0)),
        ],
        out_specs=[q_spec, q_spec, kv_spec],
        out_shape=[
            jax.ShapeDtypeStruct(queries.shape, jnp.bfloat16),
            jax.ShapeDtypeStruct(queries.shape, jnp.bfloat16),
            jax.ShapeDtypeStruct(kv.shape, jnp.bfloat16),
        ],
        scratch_shapes=[
            pltpu.VMEM((length, row_tile), jnp.float32),
            pltpu.VMEM((length, row_tile), jnp.bfloat16),
            pltpu.VMEM((2, acc_rows, width), jnp.float32),
        ],
        compiler_params=pltpu.CompilerParams(vmem_limit_bytes=60 * 1024 * 1024),
        name="attention",
    )(queries, out_grad, kv, bias)


def row_bias(rand_all, global_blocks, first, here, block_count, kv_heads):
    heads = rand_all.shape[0]
    group = heads // kv_heads
    mine = lax.dynamic_slice_in_dim(rand_all, first, here, axis=1)
    ids = first + jnp.arange(here, dtype=jnp.int32)
    key_ids = jnp.arange(block_count, dtype=jnp.int32)
    away = (key_ids[None, :] - ids[:, None] + block_count + 1) % block_count
    common = (away <= 2) | jnp.any(key_ids[None, :, None] == global_blocks[None, None, :], axis=2)
    chosen = jnp.any(mine[:, :, None, :] == key_ids[None, None, :, None], axis=3)
    live = chosen | common[None]
    bias = jnp.where(live, 0.0, -jnp.inf).astype(jnp.float32)
    bias = bias.reshape(kv_heads, group, here, block_count).transpose(0, 3, 2, 1)
    bias = jnp.broadcast_to(bias[:, :, :, None, :], (kv_heads, block_count, here, BLK, group))
    return bias.reshape(kv_heads, block_count, 1, here * BLK * group)


def fused_kernel(
    rand_in, glob_in, k_in, v_in, q_hbm, g_hbm, out_ref, dq_ref, dk_ref, dv_ref,
    grads_ref, q_buf, g_buf, kv_buf, part_buf, sib_in, right_in, left_in, right_out, left_out,
    ids_out, ids_buf, mark_buf, coarse_k, coarse_q, e_buf, ds_buf, vt_buf, kt_buf, qt_buf, gt_buf,
    q_sem, g_sem,
    ids_send, sib_send, fwd_send, back_send, far_send, pair_send, right_send, left_send,
    ids_recv, sib_recv, kv_recv, pair_recv, right_recv, left_recv,
):
    heads, _, chips, _, shard_tokens, width = kv_buf.shape
    shards = 2 * chips
    _, tokens, group, _ = q_buf.shape
    rows = tokens * group
    here = tokens // BLK
    block_count = shards * here
    lane_keys = chips * shard_tokens
    tile = 256
    tiles = rows // tile
    tile_tokens = tile // group
    chunk = 2 * shard_tokens
    chunks = shards * shard_tokens // chunk
    factor = 1.0 / math.sqrt(width)
    to_log2 = factor * math.log2(math.e)
    me = lax.axis_index("ctx")
    z, core = me // 2, me % 2
    pair = z * 2 + 1 - core
    ahead, behind = me + 2, me - 2
    last = chips - 1

    barrier = pltpu.get_barrier_semaphore()
    for k in range(1, shards):
        pl.semaphore_signal(
            barrier, inc=1, device_id={"ctx": lax.rem(me + k, shards)}, device_id_type=pl.DeviceIdType.MESH
        )

    def send(source, target, send_sem, recv_sem, to):
        return pltpu.make_async_remote_copy(
            src_ref=source, dst_ref=target, send_sem=send_sem, recv_sem=recv_sem,
            device_id={"ctx": to}, device_id_type=pl.DeviceIdType.MESH,
        )

    def send_ids(k):
        to = lax.rem(me + k, shards)
        return send(ids_out.at[to], ids_buf.at[me], ids_send, ids_recv.at[me], to)

    def got_ids(k):
        origin = lax.rem(me + k, shards)
        return send(ids_out.at[origin], ids_buf.at[origin], ids_send, ids_recv.at[origin], origin)

    def kv_spot(h, origin, w):
        return kv_buf.at[h, core, origin] if w is None else kv_buf.at[h, core, origin, w]

    def kv_move(h, origin, send_sem, to, w=None):
        spot = kv_spot(h, origin, w)
        return send(spot, spot, send_sem, kv_recv.at[heads if w == 1 else h, origin], to)

    def right_kv(h, origin, w=None):
        return kv_move(h, origin, fwd_send, ahead, w)

    def left_kv(h, origin, w=None):
        return kv_move(h, origin, back_send, behind, w)

    def sib_kv(h, origin, w=None):
        spot = kv_spot(h, origin, w)
        return send(spot, spot, sib_send, sib_recv.at[h], pair)

    def pair_move(h, w):
        return send(part_buf.at[h, w, 1 - core], sib_in.at[h, w], pair_send, pair_recv.at[h, w], pair)

    def side_move(side, h, zd, w=None):
        out, arrived = (right_out, right_in) if side == 0 else (left_out, left_in)
        sems = (right_send, right_recv) if side == 0 else (left_send, left_recv)
        at, slot = (h, zd), h
        if w is not None:
            at, slot = (h, zd, w), h + w
        return send(out.at[at], arrived.at[at], sems[0], sems[1].at[slot, zd], ahead if side == 0 else behind)

    def head_columns(ref, h):
        return ref.at[:, pl.ds(pl.multiple_of(h * group, group), group), :]

    def load_q(h):
        return pltpu.make_async_copy(head_columns(q_hbm, h), q_buf.at[h], q_sem.at[h])

    def load_g(h):
        return pltpu.make_async_copy(head_columns(g_hbm, h), g_buf.at[h], g_sem.at[h])

    def each_head(step):
        def run(h, carry):
            step(h)
            return carry
        lax.fori_loop(0, heads, run, 0)

    for which, ref in enumerate((k_in, v_in)):
        turned = jnp.swapaxes(ref[...].astype(jnp.float32), 0, 1)
        kv_buf[:, core, z, which] = turned.astype(jnp.bfloat16)

    slots = rand_in.shape[0]
    lanes = ids_buf.shape[2]
    spread = lax.broadcasted_iota(jnp.int32, (group, lanes), 1) % group
    spread = (spread == lax.broadcasted_iota(jnp.int32, (group, lanes), 0)).astype(jnp.float32)
    for k in range(slots):
        picks = lax.dot_general(
            rand_in[k].astype(jnp.float32), spread, (((0,), (0,)), ((), ())), preferred_element_type=jnp.float32
        )
        for to in range(shards):
            for b in range(here):
                spot = to * here + b
                ids_out[to, b * slots + k:b * slots + k + 1] = picks[spot:spot + 1]
    ids_buf[me] = ids_out[me]

    length = shards * shard_tokens
    spot = lax.broadcasted_iota(jnp.int32, (length, width), 0)
    spot_lane, spot_chip = spot // lane_keys, spot % lane_keys // shard_tokens
    spot_block = (spot_chip * 2 + spot_lane) * here + spot % shard_tokens // BLK
    column = lax.broadcasted_iota(jnp.int32, (length, width), 1)
    ones = jnp.logical_and(column >= block_count, column < block_count + 3)
    mark_buf[...] = jnp.logical_or(column == spot_block, ones).astype(jnp.float32).astype(jnp.bfloat16)
    coarse_k[:, width:] = jnp.where(column == spot_block, COARSE_MAX, 0.0).astype(COARSE)
    coarse_q[width:, :] = jnp.zeros((width, rows), jnp.float32).astype(COARSE)
    vt_buf[width:, :] = jnp.ones((16, length), jnp.bfloat16)
    qt_buf[width:, :] = jnp.zeros((width, rows), jnp.bfloat16)
    gt_buf[width:, :] = jnp.zeros((width, rows), jnp.bfloat16)

    pl.semaphore_wait(barrier, shards - 1)

    def own_right(h, w=None):
        @pl.when(z < last)
        def _():
            right_kv(h, z, w).start()

    def own_left(h, w=None):
        @pl.when(z > 0)
        def _():
            left_kv(h, z, w).start()

    def own_sib(h):
        sib_kv(h, z).start()

    ends = jnp.logical_or(z == 0, z == last)
    middle = jnp.logical_not(ends)

    def landed(h, origin, w=None):
        kv_move(h, origin, fwd_send, pair, w).wait_recv()

    def end_arrive(h, distance, w=None):
        origin = jnp.where(z == 0, distance, last - distance)
        landed(h, origin, w)
        sib_kv(h, origin, w).start()

    def near_arrive(h, w=None):
        landed(h, z - 1, w)
        right_kv(h, z - 1, w).start()
        sib_kv(h, z - 1, w).start()
        landed(h, z + 1, w)
        left_kv(h, z + 1, w).start()
        sib_kv(h, z + 1, w).start()

    def far_arrive(h, w=None):
        origin = jnp.where(z == 1, last, 0)
        landed(h, origin, w)
        kv_move(h, origin, far_send, jnp.where(z == 1, behind, ahead), w).start()
        sib_kv(h, origin, w).start()

    def over(low, high, step):
        def run(h, carry):
            step(h)
            return carry
        lax.fori_loop(low, high, run, 0)

    def combined(h, zd, w=None):
        at = slice(None) if w is None else w
        return part_buf[h, at, core, zd].astype(jnp.float32) + sib_in[h, at, zd].astype(jnp.float32)

    def reduce(rank, h, w=None, only=None):
        for side in range(2):
            zz = rank if side == 0 else last - rank
            targets = list(range(last, zz, -1) if side == 0 else range(zz))
            if only is not None:
                targets = targets[only:only + 1]
            out, arrived = (right_out, right_in) if side == 0 else (left_out, left_in)

            @pl.when(z == zz)
            def _(side=side, targets=targets, out=out, arrived=arrived):
                for zd in targets:
                    at = (h, zd) if w is None else (h, zd, w)
                    total = combined(h, zd, w)
                    if rank > 0:
                        side_move(side, h, zd, w).wait_recv()
                        total = total + arrived[at].astype(jnp.float32)
                    out[at] = total.astype(jnp.bfloat16)
                    side_move(side, h, zd, w).start()

    def finish(h, w=None):
        for zz in range(chips):
            @pl.when(z == zz)
            def _(zz=zz):
                at = (h, zz) if w is None else (h, zz, w)
                total = combined(h, zz, w)
                if zz > 0:
                    side_move(0, h, zz, w).wait_recv()
                    total = total + right_in[at].astype(jnp.float32)
                if zz < last:
                    side_move(1, h, zz, w).wait_recv()
                    total = total + left_in[at].astype(jnp.float32)
                for which in range(2) if w is None else (w,):
                    piece = total[which] if w is None else total
                    grads_ref[h, which] = piece.T.astype(jnp.bfloat16)

    def compute(h, hooks):
        load_q(h).wait()
        load_g(h).wait()
        ids = ids_buf[h]
        key_ids = lax.broadcasted_iota(jnp.int32, (block_count, lanes), 0)
        key_float = key_ids.astype(jnp.float32)
        for b in range(here):
            away = key_ids - (me * here + b) + (block_count + 1)
            for _ in range(2):
                away = jnp.where(away >= block_count, away - block_count, away)
            live = (away <= 2) | (key_ids == glob_in[0]) | (key_ids == glob_in[1])
            for k in range(slots):
                live = live | (key_float == ids[b * slots + k:b * slots + k + 1])
            bias = jnp.where(live, 0.0, HIDDEN).astype(jnp.float32).astype(jnp.bfloat16)
            half = rows // here
            qt_buf[width:width + block_count, b * half:(b + 1) * half] = jnp.concatenate([bias] * (half // lanes), axis=1)
            hide = jnp.where(live, 0.0, -COARSE_MAX).astype(jnp.float32)
            hide = jnp.concatenate([hide, jnp.zeros((32 - block_count, lanes), jnp.float32)], axis=0).astype(COARSE)
            coarse_q[width:width + 32, b * half:(b + 1) * half] = jnp.concatenate([hide] * (half // lanes), axis=1)

        def key_rows(which, c):
            lane, zz = c * chunk // lane_keys, c * chunk % lane_keys // shard_tokens
            return kv_buf[h, lane, zz:zz + 2, which].reshape(chunk, width)

        def columns(r):
            return slice(r * tile, (r + 1) * tile)

        def keys_at(c):
            return slice(c * chunk, (c + 1) * chunk)

        def turned_rows(ref, r):
            return ref[h, r * tile_tokens:(r + 1) * tile_tokens].reshape(tile, width).T

        def put_rows(ref, r, turned):
            block = turned.T.reshape(tile_tokens, group, width)
            ref[r * tile_tokens:(r + 1) * tile_tokens, pl.ds(pl.multiple_of(h * group, group), group), :] = block

        tops = {}

        def turn_keys(which, ref):
            for c in range(chunks):
                ref[:width, keys_at(c)] = key_rows(which, c).T

        def marked(which, at):
            spot = at.start
            keys = kv_buf[h, spot // lane_keys, spot % lane_keys // shard_tokens, which, pl.ds(spot % shard_tokens, 128)]
            return jnp.concatenate([keys, mark_buf[at]], axis=1)

        def slabs(size):
            return [slice(at, at + size) for at in range(0, length, size)]

        def coarse_keys():
            for c in range(chunks):
                coarse_k[keys_at(c), :width] = key_rows(0, c).astype(jnp.float32).astype(COARSE)

        def scores(r):
            qt = turned_rows(q_buf, r)
            qt_buf[:width, columns(r)] = qt
            coarse_q[:width, columns(r)] = qt.astype(jnp.float32).astype(COARSE)
            right = coarse_q[:, columns(r)]
            top = None
            for at in slabs(128):
                high = jnp.max(dot(coarse_k[at], right).reshape(128 // 8, 8, tile), axis=0)
                top = high if top is None else jnp.maximum(top, high)
            tops[r] = jnp.max(top, axis=0, keepdims=True) * to_log2

        def weights(r):
            right = qt_buf[:, columns(r)]
            for at in slabs(128):
                e = jnp.exp2(dot(marked(0, at), right) * to_log2 - tops[r])
                e_buf[at, columns(r)] = e.astype(jnp.bfloat16)

        def outputs(r):
            out_t = dot(vt_buf[...], e_buf[:, columns(r)])
            inverse = 1.0 / out_t[width:width + 1]
            out16 = (out_t[:width] * inverse).astype(jnp.bfloat16)
            gt = turned_rows(g_buf, r).astype(jnp.float32)
            rest = jnp.sum(gt * out16.astype(jnp.float32), axis=0, keepdims=True) * -inverse
            gt_buf[:width, columns(r)] = (gt * inverse).astype(jnp.bfloat16)
            level = lax.broadcasted_iota(jnp.int32, (16, tile), 0)
            split = jnp.zeros((16, tile), jnp.float32)
            for k in range(3):
                part = rest.astype(jnp.bfloat16).astype(jnp.float32)
                split = jnp.where(level == k, part, split)
                rest = rest - part
            gt_buf[width + block_count:width + block_count + 16, columns(r)] = split.astype(jnp.bfloat16)
            put_rows(out_ref, r, out16)

        def score_grads(r):
            right = gt_buf[:, columns(r)]
            for at in slabs(128):
                dp = dot(marked(1, at), right).astype(jnp.bfloat16)
                ds_buf[at, columns(r)] = e_buf[at, columns(r)] * dp

        def query_grads(r):
            dq_t = dot(kt_buf[...], ds_buf[:, columns(r)]) * factor
            put_rows(dq_ref, r, dq_t.astype(jnp.bfloat16))

        def key_grads(lane, w):
            left, right = ((qt_buf, ds_buf), (gt_buf, e_buf))[w]
            for zz in range(0, chips, 2):
                at = pl.ds(pl.multiple_of(lane * lane_keys + zz * shard_tokens, chunk), chunk)
                grad = dot(left[:width], right[at], NT)
                if w == 0:
                    grad = grad * factor
                grad = grad.astype(jnp.bfloat16)
                for j in range(2):
                    part_buf[h, w, lane, zz + j] = grad[:, j * shard_tokens:(j + 1) * shard_tokens]

        turn_keys(1, vt_buf)
        coarse_keys()
        scores(0)
        scores(1)
        weights(0)
        scores(2)
        weights(1)
        outputs(0)
        scores(3)
        weights(2)
        outputs(1)
        turn_keys(0, kt_buf)
        weights(3)
        outputs(2)
        outputs(3)
        key_grads(1 - core, 1)
        pair_move(h, 1).start()
        for r in range(tiles):
            score_grads(r)
        hooks[0]()
        key_grads(1 - core, 0)
        pair_move(h, 0).start()
        key_grads(core, 1)
        key_grads(core, 0)
        for r in range(tiles):
            query_grads(r)

    def lead(rank, t):
        return jnp.where(rank == 0, heads, jnp.minimum(jnp.where(rank == 1, 3 + 2 * t, 2 + t), heads))

    def start_loads(h):
        load_q(h).start()
        load_g(h).start()

    for w in range(2):
        own_right(0, w)
        own_left(0, w)
    for h in range(3):
        own_sib(h)
    for k in range(1, shards):
        send_ids(k).start()

    @pl.when(z == 0)
    def _():
        over(1, heads, own_right)

    @pl.when(z == last)
    def _():
        over(1, heads, own_left)
    each_head(start_loads)

    @pl.when(middle)
    def _():
        near_arrive(0, 0)
        near_arrive(0, 1)
        right_kv(1, z).start()
        left_kv(1, z).start()
        far_arrive(0, 0)
        far_arrive(0, 1)
        near_arrive(1)

    over(jnp.where(ends, heads, 2), lead(z, 0), own_right)
    over(jnp.where(ends, heads, 2), lead(last - z, 0), own_left)

    @pl.when(ends)
    def _():
        for distance in range(1, chips):
            end_arrive(0, distance, 0)
            end_arrive(0, distance, 1)

    for k in range(1, shards):
        got_ids(k).wait_recv()

    final = heads - 1

    def near_done(t):
        return jnp.minimum(jnp.minimum(2 + 2 * t, 4 + t), heads)

    def slot(t, carry):
        over(lead(z, t), lead(z, t + 1), own_right)
        over(lead(last - z, t), lead(last - z, t + 1), own_left)

        @pl.when(t + 3 < heads)
        def _():
            own_sib(t + 3)

        @pl.when(jnp.logical_and(middle, t == 1))
        def _():
            far_arrive(2)

        send(kv_buf.at[t, 1 - core], kv_buf.at[t, 1 - core], sib_send, sib_recv.at[t], pair).wait_recv()

        def hook():
            @pl.when(t > 0)
            def _():
                pair_move(t - 1, 1).wait_recv()
                pair_move(t - 1, 0).wait_recv()
                reduce(0, t - 1)

            @pl.when(t > 1)
            def _():
                reduce(1, t - 2)

            low = jnp.where(t == final - 1, 0, t - 3)
            over(low, jnp.where(t < final - 1, low, t - 2), lambda h: reduce(2, h))

            @pl.when(jnp.logical_and(ends, t < final))
            def _():
                for distance in range(1, chips):
                    end_arrive(t + 1, distance)

            @pl.when(middle)
            def _():
                over(near_done(t), near_done(t + 1), near_arrive)
                far = jnp.where(t == 0, 1, t + 2)
                over(far, jnp.minimum(far + 1, heads), far_arrive)

        compute(t, [hook])
        return carry

    lax.fori_loop(0, heads, slot, 0)

    reduce(1, final - 1)
    reduce(2, final - 2)
    reduce(2, final - 1)
    pair_move(final, 1).wait_recv()
    reduce(0, final, 1, 0)
    pair_move(final, 0).wait_recv()
    for rank, w, only in ((0, 0, 0), (0, 1, 1), (0, 0, 1), (0, 1, 2), (0, 0, 2),
                          (1, 1, 0), (1, 0, 0), (2, 1, 0), (1, 1, 1), (2, 0, 0), (1, 0, 1)):
        reduce(rank, final, w, only)
    over(0, final, finish)
    finish(final, 1)
    finish(final, 0)

    for which, ref in enumerate((dk_ref, dv_ref)):
        turned = jnp.swapaxes(grads_ref[:, which].astype(jnp.float32), 0, 1)
        ref[...] = turned.astype(jnp.bfloat16)

    def drained(region, sem):
        send(region, region, sem, ids_recv.at[0], pair).wait_send()

    drained(ids_out.at[pl.ds(1, shards - 1)], ids_send)
    drained(kv_buf.at[:, 0], sib_send)
    drained(sib_in, pair_send)
    @pl.when(middle)
    def _():
        drained(kv_buf.at[:, 0, pl.ds(0, 2)], fwd_send)
        drained(kv_buf.at[:, 0, pl.ds(0, 2)], back_send)
        drained(kv_buf.at[:, 0, 0], far_send)

    for zz in range(chips):
        @pl.when(z == zz)
        def _(zz=zz):
            if zz == 0:
                drained(kv_buf.at[:, 0, 0], fwd_send)
            if zz == last:
                drained(kv_buf.at[:, 0, 0], back_send)
            if zz < last:
                drained(right_out.at[:, pl.ds(0, last - zz)], right_send)
            if zz > 0:
                drained(left_out.at[:, pl.ds(0, zz)], left_send)


def fused(queries, out_grad, keys, values, rand_blocks, global_blocks, shards):
    tokens, heads, width = queries.shape
    kv_heads = keys.shape[1]
    group = heads // kv_heads
    chips = shards // 2
    rows = tokens * group
    length = tokens * shards
    blocks = length // BLK
    here = tokens // BLK
    bf16, f32 = jnp.bfloat16, jnp.float32
    vmem = pl.BlockSpec(memory_space=pltpu.VMEM)
    smem = pl.BlockSpec(memory_space=pltpu.SMEM)
    anywhere = pl.BlockSpec(memory_space=pl.ANY)
    dma = pltpu.SemaphoreType.DMA
    piece = (2, tokens, width)
    block = pltpu.VMEM((kv_heads, tokens, group, width), bf16)
    hop = pltpu.VMEM((kv_heads, chips, 2, width, tokens), bf16)
    gift = pltpu.VMEM((kv_heads, 2, chips, width, tokens), bf16)
    results = pl.pallas_call(
        fused_kernel,
        in_specs=[vmem, smem, vmem, vmem, anywhere, anywhere],
        out_specs=[vmem] * 4,
        out_shape=[
            pltpu.VMEM(queries.shape, bf16),
            pltpu.VMEM(queries.shape, bf16),
            pltpu.VMEM(keys.shape, bf16),
            pltpu.VMEM(keys.shape, bf16),
        ],
        scratch_shapes=[pltpu.VMEM((kv_heads,) + piece, bf16)] + [block] * 2
        + [
            pltpu.VMEM((kv_heads, 2, chips) + piece, bf16),
            pltpu.VMEM((kv_heads, 2, 2, chips, width, tokens), bf16),
        ]
        + [gift]
        + [hop] * 4
        + [
            pltpu.VMEM((shards, 8, 128), f32),
            pltpu.VMEM((shards, 8, 128), f32),
            pltpu.VMEM((length, 128), bf16),
            pltpu.VMEM((length, 2 * width), COARSE),
            pltpu.VMEM((2 * width, rows), COARSE),
            pltpu.VMEM((length, rows), bf16),
            pltpu.VMEM((length, rows), bf16),
            pltpu.VMEM((width + 16, length), bf16),
            pltpu.VMEM((width, length), bf16),
            pltpu.VMEM((2 * width, rows), bf16),
            pltpu.VMEM((2 * width, rows), bf16),
        ]
        + [dma((kv_heads,))] * 2
        + [dma] * 8
        + [dma((shards,)), dma((kv_heads,)), dma((kv_heads + 1, chips)), dma((kv_heads, 2))]
        + [dma((kv_heads + 1, chips))] * 2,
        compiler_params=pltpu.CompilerParams(
            collective_id=0, has_side_effects=True, vmem_limit_bytes=50 * 1024 * 1024
        ),
        name="fused",
    )(rand_blocks.transpose(2, 0, 1), global_blocks, keys, values, queries, out_grad)
    return settle(results)


def settle(arrays):
    count = len(arrays)

    def kernel(*refs):
        copies = [pltpu.make_async_copy(refs[i], refs[count + i], refs[2 * count].at[i]) for i in range(count)]
        for copy in copies:
            copy.start()
        for copy in copies:
            copy.wait()

    anywhere = pl.BlockSpec(memory_space=pl.ANY)
    return pl.pallas_call(
        kernel,
        in_specs=[pl.BlockSpec(memory_space=pltpu.VMEM)] * count,
        out_specs=[pl.BlockSpec(memory_space=pltpu.HBM)] * count,
        out_shape=[jax.ShapeDtypeStruct(a.shape, a.dtype) for a in arrays],
        scratch_shapes=[pltpu.SemaphoreType.DMA((count,))],
        compiler_params=pltpu.CompilerParams(vmem_limit_bytes=1 << 20),
        name="settle",
    )(*[pltpu.with_memory_space_constraint(a, pltpu.VMEM) for a in arrays])


def body(shards, queries, keys, values, out_grad, rand_blocks, global_blocks):
    tokens, kv_heads, width = keys.shape
    here = tokens // BLK
    block_count = rand_blocks.shape[1]
    group = queries.shape[1] // kv_heads
    me = lax.axis_index("ctx")
    if (shards == kv_heads == group == 8 and here == 2 and rand_blocks.shape[2] == 3
            and global_blocks.shape[0] == 2):
        return fused(queries, out_grad, keys, values, rand_blocks, global_blocks, shards)
    kv_here = jnp.stack([keys.transpose(1, 0, 2), values.transpose(1, 0, 2)], axis=1)
    kv = lax.all_gather(kv_here, "ctx", axis=0)
    rand_all = lax.all_gather(rand_blocks, "ctx", axis=0, tiled=True)
    bias = row_bias(rand_all, global_blocks, me * here, here, block_count, kv_heads)
    output, query_grad, parts = local_attention(queries, out_grad, kv, bias)
    sums = lax.psum_scatter(parts, "ctx", scatter_dimension=0, tiled=False)
    grads = sums.transpose(1, 2, 0, 3)
    return output, query_grad, grads[0], grads[1]


def solution(mesh):
    split = P(("dp", "ctx"), None, None)
    return jax.shard_map(
        functools.partial(body, mesh.shape["ctx"]),
        mesh=mesh,
        in_specs=(split, split, split, split, split, P("dp")),
        out_specs=(split, split, split, split),
        check_vma=False,
    )
```

```python
import functools
import math

import jax
import jax.numpy as jnp
from jax import lax
from jax.experimental import pallas as pl
from jax.experimental.pallas import tpu as pltpu
from jax.sharding import PartitionSpec as P

BLK = 64
NT = (((1,), (1,)), ((), ()))
NN = (((1,), (0,)), ((), ()))
HIDDEN = -1e30
COARSE = jnp.float8_e4m3fn
COARSE_MAX = 448.0


def dot(left, right, dims=NN):
    return lax.dot_general(left, right, dims, preferred_element_type=jnp.float32)


def flat_rows(block):
    rows = block.shape[0] * block.shape[1]
    return block.astype(jnp.float32).reshape(rows, block.shape[2])


def for_chunks(count, step, init):
    return lax.fori_loop(0, count, step, init, unroll=count <= 4)


def attention(geometry, q_ref, g_ref, kv_ref, bias_ref, out_ref, dq_ref, dkv_ref, s_buf, e_buf, acc):
    chunk, row_tile = geometry
    shards, _, _, shard_tokens, width = kv_ref.shape
    length = shards * shard_tokens
    count = length // chunk
    tokens, group, _ = q_ref.shape
    rows = tokens * group
    tiles = rows // row_tile
    tile_tokens = row_tile // group
    factor = 1.0 / math.sqrt(width)
    to_log2 = factor * math.log2(math.e)
    per_chunk = chunk // shard_tokens

    def kv_chunk(which, c):
        return kv_ref[pl.ds(c * per_chunk, per_chunk), 0, which].reshape(chunk, width)

    for tile in range(tiles):
        t0 = tile * tile_tokens
        lanes = pl.ds(tile * row_tile, row_tile)
        q = flat_rows(q_ref[pl.ds(t0, tile_tokens)]).astype(jnp.bfloat16)
        g32 = flat_rows(g_ref[pl.ds(t0, tile_tokens)])

        def score_step(c, top):
            s = dot(kv_chunk(0, c), q, NT) * to_log2
            blocks = chunk // BLK
            bias = bias_ref[0, pl.ds(c * blocks, blocks), :, lanes]
            s = (s.reshape(blocks, BLK, row_tile) + bias).reshape(chunk, row_tile)
            s_buf[pl.ds(c * chunk, chunk)] = s
            return jnp.maximum(top, jnp.max(s, axis=0, keepdims=True))

        top = for_chunks(count, score_step, jnp.full((1, row_tile), -jnp.inf, jnp.float32))

        def weight_step(c, carry):
            total, out_t = carry
            e = jnp.exp2(s_buf[pl.ds(c * chunk, chunk)] - top)
            total = total + jnp.sum(e, axis=0, keepdims=True)
            e16 = e.astype(jnp.bfloat16)
            e_buf[pl.ds(c * chunk, chunk)] = e16
            out_t = out_t + dot(kv_chunk(1, c).T, e16)
            return total, out_t

        total, out_t = for_chunks(
            count,
            weight_step,
            (jnp.zeros((1, row_tile), jnp.float32), jnp.zeros((width, row_tile), jnp.float32)),
        )
        inverse = 1.0 / total
        out16 = (out_t * inverse).T.astype(jnp.bfloat16)
        out32 = out16.astype(jnp.float32)
        out_ref[pl.ds(t0, tile_tokens)] = out32.reshape(tile_tokens, group, width).astype(jnp.bfloat16)
        delta = jnp.sum((g32 * out32).T, axis=0, keepdims=True) * inverse
        g16 = (g32.T * inverse).T.astype(jnp.bfloat16)

        def grad_step(c, dq_t):
            at = pl.ds(c * chunk, chunk)
            e16 = e_buf[at]
            dp = dot(kv_chunk(1, c), g16, NT)
            ds = (e16.astype(jnp.float32) * (dp - delta)).astype(jnp.bfloat16)
            dk = dot(ds, q)
            dv = dot(e16, g16)
            if tile > 0:
                dk = dk + acc[0, at]
                dv = dv + acc[1, at]
            if tile < tiles - 1:
                acc[0, at] = dk
                acc[1, at] = dv
            else:
                shape = (per_chunk, shard_tokens, width)
                spot = pl.ds(c * per_chunk, per_chunk)
                dkv_ref[spot, 0, 0] = (dk * factor).astype(jnp.bfloat16).reshape(shape)
                dkv_ref[spot, 0, 1] = dv.astype(jnp.bfloat16).reshape(shape)
            return dq_t + dot(kv_chunk(0, c).T, ds)

        dq_t = for_chunks(count, grad_step, jnp.zeros((width, row_tile), jnp.float32))
        dq = (dq_t * factor).T.reshape(tile_tokens, group, width)
        dq_ref[pl.ds(t0, tile_tokens)] = dq.astype(jnp.bfloat16)


def local_attention(queries, out_grad, kv, bias):
    tokens, heads, width = queries.shape
    shards, kv_heads, _, shard_tokens, _ = kv.shape
    group = heads // kv_heads
    length = shards * shard_tokens
    rows = tokens * group
    chunk = math.gcd(length, 256)
    row_tile = rows
    while row_tile * length > (1 << 21) and row_tile > 128:
        row_tile //= 2
    acc_rows = length if row_tile < rows else 8
    blocks = length // BLK
    q_spec = pl.BlockSpec((tokens, group, width), lambda g: (0, g, 0))
    kv_spec = pl.BlockSpec((shards, 1, 2, shard_tokens, width), lambda g: (0, g, 0, 0, 0))
    return pl.pallas_call(
        functools.partial(attention, (chunk, row_tile)),
        grid=(kv_heads,),
        in_specs=[
            q_spec,
            q_spec,
            kv_spec,
            pl.BlockSpec((1, blocks, 1, rows), lambda g: (g, 0, 0, 0)),
        ],
        out_specs=[q_spec, q_spec, kv_spec],
        out_shape=[
            jax.ShapeDtypeStruct(queries.shape, jnp.bfloat16),
            jax.ShapeDtypeStruct(queries.shape, jnp.bfloat16),
            jax.ShapeDtypeStruct(kv.shape, jnp.bfloat16),
        ],
        scratch_shapes=[
            pltpu.VMEM((length, row_tile), jnp.float32),
            pltpu.VMEM((length, row_tile), jnp.bfloat16),
            pltpu.VMEM((2, acc_rows, width), jnp.float32),
        ],
        compiler_params=pltpu.CompilerParams(vmem_limit_bytes=60 * 1024 * 1024),
        name="attention",
    )(queries, out_grad, kv, bias)


def row_bias(rand_all, global_blocks, first, here, block_count, kv_heads):
    heads = rand_all.shape[0]
    group = heads // kv_heads
    mine = lax.dynamic_slice_in_dim(rand_all, first, here, axis=1)
    ids = first + jnp.arange(here, dtype=jnp.int32)
    key_ids = jnp.arange(block_count, dtype=jnp.int32)
    away = (key_ids[None, :] - ids[:, None] + block_count + 1) % block_count
    common = (away <= 2) | jnp.any(key_ids[None, :, None] == global_blocks[None, None, :], axis=2)
    chosen = jnp.any(mine[:, :, None, :] == key_ids[None, None, :, None], axis=3)
    live = chosen | common[None]
    bias = jnp.where(live, 0.0, -jnp.inf).astype(jnp.float32)
    bias = bias.reshape(kv_heads, group, here, block_count).transpose(0, 3, 2, 1)
    bias = jnp.broadcast_to(bias[:, :, :, None, :], (kv_heads, block_count, here, BLK, group))
    return bias.reshape(kv_heads, block_count, 1, here * BLK * group)


def fused_kernel(
    rand_in, glob_in, k_in, v_in, q_hbm, g_hbm, out_ref, dq_ref, dk_ref, dv_ref,
    grads_ref, q_buf, g_buf, kv_buf, part_buf, sib_in, right_in, left_in, right_out, left_out,
    ids_out, ids_buf, mark_buf, coarse_k, coarse_q, e_buf, ds_buf, vt_buf, kt_buf, qt_buf, gt_buf,
    q_sem, g_sem,
    ids_send, sib_send, fwd_send, back_send, far_send, pair_send, right_send, left_send,
    ids_recv, sib_recv, kv_recv, pair_recv, right_recv, left_recv,
):
    heads, _, chips, _, shard_tokens, width = kv_buf.shape
    shards = 2 * chips
    _, tokens, group, _ = q_buf.shape
    rows = tokens * group
    here = tokens // BLK
    block_count = shards * here
    lane_keys = chips * shard_tokens
    tile = 256
    tiles = rows // tile
    tile_tokens = tile // group
    chunk = 2 * shard_tokens
    chunks = shards * shard_tokens // chunk
    factor = 1.0 / math.sqrt(width)
    to_log2 = factor * math.log2(math.e)
    me = lax.axis_index("ctx")
    z, core = me // 2, me % 2
    pair = z * 2 + 1 - core
    ahead, behind = me + 2, me - 2
    last = chips - 1

    barrier = pltpu.get_barrier_semaphore()
    for k in range(1, shards):
        pl.semaphore_signal(
            barrier, inc=1, device_id={"ctx": lax.rem(me + k, shards)}, device_id_type=pl.DeviceIdType.MESH
        )

    def send(source, target, send_sem, recv_sem, to):
        return pltpu.make_async_remote_copy(
            src_ref=source, dst_ref=target, send_sem=send_sem, recv_sem=recv_sem,
            device_id={"ctx": to}, device_id_type=pl.DeviceIdType.MESH,
        )

    def send_ids(k):
        to = lax.rem(me + k, shards)
        return send(ids_out.at[to], ids_buf.at[me], ids_send, ids_recv.at[me], to)

    def got_ids(k):
        origin = lax.rem(me + k, shards)
        return send(ids_out.at[origin], ids_buf.at[origin], ids_send, ids_recv.at[origin], origin)

    def kv_spot(h, origin, w):
        return kv_buf.at[h, core, origin] if w is None else kv_buf.at[h, core, origin, w]

    def kv_move(h, origin, send_sem, to, w=None):
        spot = kv_spot(h, origin, w)
        return send(spot, spot, send_sem, kv_recv.at[heads if w == 1 else h, origin], to)

    def right_kv(h, origin, w=None):
        return kv_move(h, origin, fwd_send, ahead, w)

    def left_kv(h, origin, w=None):
        return kv_move(h, origin, back_send, behind, w)

    def sib_kv(h, origin, w=None):
        spot = kv_spot(h, origin, w)
        return send(spot, spot, sib_send, sib_recv.at[h], pair)

    def pair_move(h, w):
        return send(part_buf.at[h, w, 1 - core], sib_in.at[h, w], pair_send, pair_recv.at[h, w], pair)

    def side_move(side, h, zd, w=None):
        out, arrived = (right_out, right_in) if side == 0 else (left_out, left_in)
        sems = (right_send, right_recv) if side == 0 else (left_send, left_recv)
        at, slot = (h, zd), h
        if w is not None:
            at, slot = (h, zd, w), h + w
        return send(out.at[at], arrived.at[at], sems[0], sems[1].at[slot, zd], ahead if side == 0 else behind)

    def head_columns(ref, h):
        return ref.at[:, pl.ds(pl.multiple_of(h * group, group), group), :]

    def load_q(h):
        return pltpu.make_async_copy(head_columns(q_hbm, h), q_buf.at[h], q_sem.at[h])

    def load_g(h):
        return pltpu.make_async_copy(head_columns(g_hbm, h), g_buf.at[h], g_sem.at[h])

    def each_head(step):
        def run(h, carry):
            step(h)
            return carry
        lax.fori_loop(0, heads, run, 0)

    for which, ref in enumerate((k_in, v_in)):
        turned = jnp.swapaxes(ref[...].astype(jnp.float32), 0, 1)
        kv_buf[:, core, z, which] = turned.astype(jnp.bfloat16)

    slots = rand_in.shape[0]
    lanes = ids_buf.shape[2]
    spread = lax.broadcasted_iota(jnp.int32, (group, lanes), 1) % group
    spread = (spread == lax.broadcasted_iota(jnp.int32, (group, lanes), 0)).astype(jnp.float32)
    for k in range(slots):
        picks = lax.dot_general(
            rand_in[k].astype(jnp.float32), spread, (((0,), (0,)), ((), ())), preferred_element_type=jnp.float32
        )
        for to in range(shards):
            for b in range(here):
                spot = to * here + b
                ids_out[to, b * slots + k:b * slots + k + 1] = picks[spot:spot + 1]
    ids_buf[me] = ids_out[me]

    length = shards * shard_tokens
    spot = lax.broadcasted_iota(jnp.int32, (length, width), 0)
    spot_lane, spot_chip = spot // lane_keys, spot % lane_keys // shard_tokens
    spot_block = (spot_chip * 2 + spot_lane) * here + spot % shard_tokens // BLK
    column = lax.broadcasted_iota(jnp.int32, (length, width), 1)
    ones = jnp.logical_and(column >= block_count, column < block_count + 3)
    mark_buf[...] = jnp.logical_or(column == spot_block, ones).astype(jnp.float32).astype(jnp.bfloat16)
    coarse_k[:, width:] = jnp.where(column == spot_block, COARSE_MAX, 0.0).astype(COARSE)
    coarse_q[width:, :] = jnp.zeros((width, rows), jnp.float32).astype(COARSE)
    vt_buf[width:, :] = jnp.ones((16, length), jnp.bfloat16)
    qt_buf[width:, :] = jnp.zeros((width, rows), jnp.bfloat16)
    gt_buf[width:, :] = jnp.zeros((width, rows), jnp.bfloat16)

    pl.semaphore_wait(barrier, shards - 1)

    def own_right(h, w=None):
        @pl.when(z < last)
        def _():
            right_kv(h, z, w).start()

    def own_left(h, w=None):
        @pl.when(z > 0)
        def _():
            left_kv(h, z, w).start()

    def own_sib(h):
        sib_kv(h, z).start()

    ends = jnp.logical_or(z == 0, z == last)
    middle = jnp.logical_not(ends)

    def landed(h, origin, w=None):
        kv_move(h, origin, fwd_send, pair, w).wait_recv()

    def end_arrive(h, distance, w=None):
        origin = jnp.where(z == 0, distance, last - distance)
        landed(h, origin, w)
        sib_kv(h, origin, w).start()

    def near_arrive(h, w=None):
        landed(h, z - 1, w)
        right_kv(h, z - 1, w).start()
        sib_kv(h, z - 1, w).start()
        landed(h, z + 1, w)
        left_kv(h, z + 1, w).start()
        sib_kv(h, z + 1, w).start()

    def far_arrive(h, w=None):
        origin = jnp.where(z == 1, last, 0)
        landed(h, origin, w)
        kv_move(h, origin, far_send, jnp.where(z == 1, behind, ahead), w).start()
        sib_kv(h, origin, w).start()

    def over(low, high, step):
        def run(h, carry):
            step(h)
            return carry
        lax.fori_loop(low, high, run, 0)

    def combined(h, zd, w=None):
        at = slice(None) if w is None else w
        return part_buf[h, at, core, zd].astype(jnp.float32) + sib_in[h, at, zd].astype(jnp.float32)

    def reduce(rank, h, w=None, only=None):
        for side in range(2):
            zz = rank if side == 0 else last - rank
            targets = list(range(last, zz, -1) if side == 0 else range(zz))
            if only is not None:
                targets = targets[only:only + 1]
            out, arrived = (right_out, right_in) if side == 0 else (left_out, left_in)

            @pl.when(z == zz)
            def _(side=side, targets=targets, out=out, arrived=arrived):
                for zd in targets:
                    at = (h, zd) if w is None else (h, zd, w)
                    total = combined(h, zd, w)
                    if rank > 0:
                        side_move(side, h, zd, w).wait_recv()
                        total = total + arrived[at].astype(jnp.float32)
                    out[at] = total.astype(jnp.bfloat16)
                    side_move(side, h, zd, w).start()

    def finish(h, w=None):
        for zz in range(chips):
            @pl.when(z == zz)
            def _(zz=zz):
                at = (h, zz) if w is None else (h, zz, w)
                total = combined(h, zz, w)
                if zz > 0:
                    side_move(0, h, zz, w).wait_recv()
                    total = total + right_in[at].astype(jnp.float32)
                if zz < last:
                    side_move(1, h, zz, w).wait_recv()
                    total = total + left_in[at].astype(jnp.float32)
                for which in range(2) if w is None else (w,):
                    piece = total[which] if w is None else total
                    grads_ref[h, which] = piece.T.astype(jnp.bfloat16)

    def compute(h, hooks):
        load_q(h).wait()
        load_g(h).wait()
        ids = ids_buf[h]
        key_ids = lax.broadcasted_iota(jnp.int32, (block_count, lanes), 0)
        key_float = key_ids.astype(jnp.float32)
        for b in range(here):
            away = key_ids - (me * here + b) + (block_count + 1)
            for _ in range(2):
                away = jnp.where(away >= block_count, away - block_count, away)
            live = (away <= 2) | (key_ids == glob_in[0]) | (key_ids == glob_in[1])
            for k in range(slots):
                live = live | (key_float == ids[b * slots + k:b * slots + k + 1])
            bias = jnp.where(live, 0.0, HIDDEN).astype(jnp.float32).astype(jnp.bfloat16)
            half = rows // here
            qt_buf[width:width + block_count, b * half:(b + 1) * half] = jnp.concatenate([bias] * (half // lanes), axis=1)
            hide = jnp.where(live, 0.0, -COARSE_MAX).astype(jnp.float32)
            hide = jnp.concatenate([hide, jnp.zeros((32 - block_count, lanes), jnp.float32)], axis=0).astype(COARSE)
            coarse_q[width:width + 32, b * half:(b + 1) * half] = jnp.concatenate([hide] * (half // lanes), axis=1)

        def key_rows(which, c):
            lane, zz = c * chunk // lane_keys, c * chunk % lane_keys // shard_tokens
            return kv_buf[h, lane, zz:zz + 2, which].reshape(chunk, width)

        def columns(r):
            return slice(r * tile, (r + 1) * tile)

        def keys_at(c):
            return slice(c * chunk, (c + 1) * chunk)

        def turned_rows(ref, r):
            return ref[h, r * tile_tokens:(r + 1) * tile_tokens].reshape(tile, width).T

        def put_rows(ref, r, turned):
            block = turned.T.reshape(tile_tokens, group, width)
            ref[r * tile_tokens:(r + 1) * tile_tokens, pl.ds(pl.multiple_of(h * group, group), group), :] = block

        tops = {}

        def turn_keys(which, ref):
            for c in range(chunks):
                ref[:width, keys_at(c)] = key_rows(which, c).T

        def marked(which, at):
            size, spot = at.stop - at.start, at.start
            lane, zz = spot // lane_keys, spot % lane_keys // shard_tokens
            keys = kv_buf[h, lane, zz:zz + size // shard_tokens, which].reshape(size, width)
            return jnp.concatenate([keys, mark_buf[at]], axis=1)

        def slabs(size):
            return [slice(at, at + size) for at in range(0, length, size)]

        def coarse_keys():
            for c in range(chunks):
                coarse_k[keys_at(c), :width] = key_rows(0, c).astype(jnp.float32).astype(COARSE)

        def scores(r):
            qt = turned_rows(q_buf, r)
            qt_buf[:width, columns(r)] = qt
            coarse_q[:width, columns(r)] = qt.astype(jnp.float32).astype(COARSE)
            right = coarse_q[:, columns(r)]
            top = None
            for at in slabs(512):
                high = jnp.max(dot(coarse_k[at], right).reshape(512 // 8, 8, tile), axis=0)
                top = high if top is None else jnp.maximum(top, high)
            tops[r] = jnp.max(top, axis=0, keepdims=True) * to_log2

        def weights(r):
            right = qt_buf[:, columns(r)]
            for at in slabs(512):
                e = jnp.exp2(dot(marked(0, at), right) * to_log2 - tops[r])
                e_buf[at, columns(r)] = e.astype(jnp.bfloat16)

        def outputs(r):
            out_t = dot(vt_buf[...], e_buf[:, columns(r)])
            inverse = 1.0 / out_t[width:width + 1]
            out16 = (out_t[:width] * inverse).astype(jnp.bfloat16)
            gt = turned_rows(g_buf, r).astype(jnp.float32)
            rest = jnp.sum(gt * out16.astype(jnp.float32), axis=0, keepdims=True) * -inverse
            gt_buf[:width, columns(r)] = (gt * inverse).astype(jnp.bfloat16)
            level = lax.broadcasted_iota(jnp.int32, (16, tile), 0)
            split = jnp.zeros((16, tile), jnp.float32)
            for k in range(3):
                part = rest.astype(jnp.bfloat16).astype(jnp.float32)
                split = jnp.where(level == k, part, split)
                rest = rest - part
            gt_buf[width + block_count:width + block_count + 16, columns(r)] = split.astype(jnp.bfloat16)
            put_rows(out_ref, r, out16)

        def score_grads(r):
            right = gt_buf[:, columns(r)]
            for at in slabs(512):
                dp = dot(marked(1, at), right).astype(jnp.bfloat16)
                ds_buf[at, columns(r)] = e_buf[at, columns(r)] * dp

        def query_grads(r):
            dq_t = dot(kt_buf[...], ds_buf[:, columns(r)]) * factor
            put_rows(dq_ref, r, dq_t.astype(jnp.bfloat16))

        def key_grads(lane, w):
            left, right = ((qt_buf, ds_buf), (gt_buf, e_buf))[w]
            for zz in range(0, chips, 2):
                at = pl.ds(pl.multiple_of(lane * lane_keys + zz * shard_tokens, chunk), chunk)
                grad = dot(left[:width], right[at], NT)
                if w == 0:
                    grad = grad * factor
                grad = grad.astype(jnp.bfloat16)
                for j in range(2):
                    part_buf[h, w, lane, zz + j] = grad[:, j * shard_tokens:(j + 1) * shard_tokens]

        turn_keys(1, vt_buf)
        coarse_keys()
        scores(0)
        scores(1)
        weights(0)
        scores(2)
        weights(1)
        outputs(0)
        scores(3)
        weights(2)
        outputs(1)
        turn_keys(0, kt_buf)
        weights(3)
        outputs(2)
        outputs(3)
        key_grads(1 - core, 1)
        pair_move(h, 1).start()
        for r in range(tiles):
            score_grads(r)
        hooks[0]()
        key_grads(1 - core, 0)
        pair_move(h, 0).start()
        key_grads(core, 1)
        key_grads(core, 0)
        for r in range(tiles):
            query_grads(r)

    def lead(rank, t):
        return jnp.where(rank == 0, heads, jnp.minimum(jnp.where(rank == 1, 3 + 2 * t, 2 + t), heads))

    def start_loads(h):
        load_q(h).start()
        load_g(h).start()

    for w in range(2):
        own_right(0, w)
        own_left(0, w)
    for h in range(3):
        own_sib(h)
    for k in range(1, shards):
        send_ids(k).start()

    @pl.when(z == 0)
    def _():
        over(1, heads, own_right)

    @pl.when(z == last)
    def _():
        over(1, heads, own_left)
    each_head(start_loads)

    @pl.when(middle)
    def _():
        near_arrive(0, 0)
        near_arrive(0, 1)
        right_kv(1, z).start()
        left_kv(1, z).start()
        far_arrive(0, 0)
        far_arrive(0, 1)
        near_arrive(1)

    over(jnp.where(ends, heads, 2), lead(z, 0), own_right)
    over(jnp.where(ends, heads, 2), lead(last - z, 0), own_left)

    @pl.when(ends)
    def _():
        for distance in range(1, chips):
            end_arrive(0, distance, 0)
            end_arrive(0, distance, 1)

    for k in range(1, shards):
        got_ids(k).wait_recv()

    final = heads - 1

    def near_done(t):
        return jnp.minimum(jnp.minimum(2 + 2 * t, 4 + t), heads)

    def slot(t, carry):
        over(lead(z, t), lead(z, t + 1), own_right)
        over(lead(last - z, t), lead(last - z, t + 1), own_left)

        @pl.when(t + 3 < heads)
        def _():
            own_sib(t + 3)

        @pl.when(jnp.logical_and(middle, t == 1))
        def _():
            far_arrive(2)

        send(kv_buf.at[t, 1 - core], kv_buf.at[t, 1 - core], sib_send, sib_recv.at[t], pair).wait_recv()

        def hook():
            @pl.when(jnp.logical_and(ends, t < final))
            def _():
                for distance in range(1, chips):
                    end_arrive(t + 1, distance)

            @pl.when(middle)
            def _():
                far = jnp.where(t == 0, 1, t + 2)
                over(far, jnp.minimum(far + 1, heads), far_arrive)
                over(near_done(t), near_done(t + 1), near_arrive)

            @pl.when(t > 0)
            def _():
                pair_move(t - 1, 1).wait_recv()
                pair_move(t - 1, 0).wait_recv()
                reduce(0, t - 1)

            @pl.when(t > 1)
            def _():
                reduce(1, t - 2)

            low = jnp.where(t == final - 1, 0, t - 3)
            over(low, jnp.where(t < final - 1, low, t - 2), lambda h: reduce(2, h))

        compute(t, [hook])
        return carry

    lax.fori_loop(0, heads, slot, 0)

    reduce(1, final - 1)
    reduce(2, final - 2)
    reduce(2, final - 1)
    pair_move(final, 1).wait_recv()
    reduce(0, final, 1, 0)
    pair_move(final, 0).wait_recv()
    for rank, w, only in ((0, 0, 0), (0, 1, 1), (0, 0, 1), (0, 1, 2), (0, 0, 2),
                          (1, 1, 0), (1, 0, 0), (2, 1, 0), (1, 1, 1), (2, 0, 0), (1, 0, 1)):
        reduce(rank, final, w, only)
    over(0, final, finish)
    finish(final, 1)
    finish(final, 0)

    for which, ref in enumerate((dk_ref, dv_ref)):
        turned = jnp.swapaxes(grads_ref[:, which].astype(jnp.float32), 0, 1)
        ref[...] = turned.astype(jnp.bfloat16)

    def drained(region, sem):
        send(region, region, sem, ids_recv.at[0], pair).wait_send()

    drained(ids_out.at[pl.ds(1, shards - 1)], ids_send)
    drained(kv_buf.at[:, 0], sib_send)
    drained(sib_in, pair_send)
    @pl.when(middle)
    def _():
        drained(kv_buf.at[:, 0, pl.ds(0, 2)], fwd_send)
        drained(kv_buf.at[:, 0, pl.ds(0, 2)], back_send)
        drained(kv_buf.at[:, 0, 0], far_send)

    for zz in range(chips):
        @pl.when(z == zz)
        def _(zz=zz):
            if zz == 0:
                drained(kv_buf.at[:, 0, 0], fwd_send)
            if zz == last:
                drained(kv_buf.at[:, 0, 0], back_send)
            if zz < last:
                drained(right_out.at[:, pl.ds(0, last - zz)], right_send)
            if zz > 0:
                drained(left_out.at[:, pl.ds(0, zz)], left_send)


def fused(queries, out_grad, keys, values, rand_blocks, global_blocks, shards):
    tokens, heads, width = queries.shape
    kv_heads = keys.shape[1]
    group = heads // kv_heads
    chips = shards // 2
    rows = tokens * group
    length = tokens * shards
    blocks = length // BLK
    here = tokens // BLK
    bf16, f32 = jnp.bfloat16, jnp.float32
    vmem = pl.BlockSpec(memory_space=pltpu.VMEM)
    smem = pl.BlockSpec(memory_space=pltpu.SMEM)
    anywhere = pl.BlockSpec(memory_space=pl.ANY)
    dma = pltpu.SemaphoreType.DMA
    piece = (2, tokens, width)
    block = pltpu.VMEM((kv_heads, tokens, group, width), bf16)
    hop = pltpu.VMEM((kv_heads, chips, 2, width, tokens), bf16)
    gift = pltpu.VMEM((kv_heads, 2, chips, width, tokens), bf16)
    results = pl.pallas_call(
        fused_kernel,
        in_specs=[vmem, smem, vmem, vmem, anywhere, anywhere],
        out_specs=[vmem] * 4,
        out_shape=[
            pltpu.VMEM(queries.shape, bf16),
            pltpu.VMEM(queries.shape, bf16),
            pltpu.VMEM(keys.shape, bf16),
            pltpu.VMEM(keys.shape, bf16),
        ],
        scratch_shapes=[pltpu.VMEM((kv_heads,) + piece, bf16)] + [block] * 2
        + [
            pltpu.VMEM((kv_heads, 2, chips) + piece, bf16),
            pltpu.VMEM((kv_heads, 2, 2, chips, width, tokens), bf16),
        ]
        + [gift]
        + [hop] * 4
        + [
            pltpu.VMEM((shards, 8, 128), f32),
            pltpu.VMEM((shards, 8, 128), f32),
            pltpu.VMEM((length, 128), bf16),
            pltpu.VMEM((length, 2 * width), COARSE),
            pltpu.VMEM((2 * width, rows), COARSE),
            pltpu.VMEM((length, rows), bf16),
            pltpu.VMEM((length, rows), bf16),
            pltpu.VMEM((width + 16, length), bf16),
            pltpu.VMEM((width, length), bf16),
            pltpu.VMEM((2 * width, rows), bf16),
            pltpu.VMEM((2 * width, rows), bf16),
        ]
        + [dma((kv_heads,))] * 2
        + [dma] * 8
        + [dma((shards,)), dma((kv_heads,)), dma((kv_heads + 1, chips)), dma((kv_heads, 2))]
        + [dma((kv_heads + 1, chips))] * 2,
        compiler_params=pltpu.CompilerParams(
            collective_id=0, has_side_effects=True, vmem_limit_bytes=50 * 1024 * 1024
        ),
        name="fused",
    )(rand_blocks.transpose(2, 0, 1), global_blocks, keys, values, queries, out_grad)
    return settle(results)


def settle(arrays):
    count = len(arrays)

    def kernel(*refs):
        copies = [pltpu.make_async_copy(refs[i], refs[count + i], refs[2 * count].at[i]) for i in range(count)]
        for copy in copies:
            copy.start()
        for copy in copies:
            copy.wait()

    anywhere = pl.BlockSpec(memory_space=pl.ANY)
    return pl.pallas_call(
        kernel,
        in_specs=[pl.BlockSpec(memory_space=pltpu.VMEM)] * count,
        out_specs=[pl.BlockSpec(memory_space=pltpu.HBM)] * count,
        out_shape=[jax.ShapeDtypeStruct(a.shape, a.dtype) for a in arrays],
        scratch_shapes=[pltpu.SemaphoreType.DMA((count,))],
        compiler_params=pltpu.CompilerParams(vmem_limit_bytes=1 << 20),
        name="settle",
    )(*[pltpu.with_memory_space_constraint(a, pltpu.VMEM) for a in arrays])


def body(shards, queries, keys, values, out_grad, rand_blocks, global_blocks):
    tokens, kv_heads, width = keys.shape
    here = tokens // BLK
    block_count = rand_blocks.shape[1]
    group = queries.shape[1] // kv_heads
    me = lax.axis_index("ctx")
    if (shards == kv_heads == group == 8 and here == 2 and rand_blocks.shape[2] == 3
            and global_blocks.shape[0] == 2):
        return fused(queries, out_grad, keys, values, rand_blocks, global_blocks, shards)
    kv_here = jnp.stack([keys.transpose(1, 0, 2), values.transpose(1, 0, 2)], axis=1)
    kv = lax.all_gather(kv_here, "ctx", axis=0)
    rand_all = lax.all_gather(rand_blocks, "ctx", axis=0, tiled=True)
    bias = row_bias(rand_all, global_blocks, me * here, here, block_count, kv_heads)
    output, query_grad, parts = local_attention(queries, out_grad, kv, bias)
    sums = lax.psum_scatter(parts, "ctx", scatter_dimension=0, tiled=False)
    grads = sums.transpose(1, 2, 0, 3)
    return output, query_grad, grads[0], grads[1]


def solution(mesh):
    split = P(("dp", "ctx"), None, None)
    return jax.shard_map(
        functools.partial(body, mesh.shape["ctx"]),
        mesh=mesh,
        in_specs=(split, split, split, split, split, P("dp")),
        out_specs=(split, split, split, split),
        check_vma=False,
    )
```

```python
import functools
import math

import jax
import jax.numpy as jnp
from jax import lax
from jax.experimental import pallas as pl
from jax.experimental.pallas import tpu as pltpu
from jax.sharding import PartitionSpec as P

BLK = 64
NT = (((1,), (1,)), ((), ()))
NN = (((1,), (0,)), ((), ()))
HIDDEN = -1e30
COARSE = jnp.float8_e4m3fn
COARSE_MAX = 448.0


def dot(left, right, dims=NN):
    return lax.dot_general(left, right, dims, preferred_element_type=jnp.float32)


def flat_rows(block):
    rows = block.shape[0] * block.shape[1]
    return block.astype(jnp.float32).reshape(rows, block.shape[2])


def for_chunks(count, step, init):
    return lax.fori_loop(0, count, step, init, unroll=count <= 4)


def attention(geometry, q_ref, g_ref, kv_ref, bias_ref, out_ref, dq_ref, dkv_ref, s_buf, e_buf, acc):
    chunk, row_tile = geometry
    shards, _, _, shard_tokens, width = kv_ref.shape
    length = shards * shard_tokens
    count = length // chunk
    tokens, group, _ = q_ref.shape
    rows = tokens * group
    tiles = rows // row_tile
    tile_tokens = row_tile // group
    factor = 1.0 / math.sqrt(width)
    to_log2 = factor * math.log2(math.e)
    per_chunk = chunk // shard_tokens

    def kv_chunk(which, c):
        return kv_ref[pl.ds(c * per_chunk, per_chunk), 0, which].reshape(chunk, width)

    for tile in range(tiles):
        t0 = tile * tile_tokens
        lanes = pl.ds(tile * row_tile, row_tile)
        q = flat_rows(q_ref[pl.ds(t0, tile_tokens)]).astype(jnp.bfloat16)
        g32 = flat_rows(g_ref[pl.ds(t0, tile_tokens)])

        def score_step(c, top):
            s = dot(kv_chunk(0, c), q, NT) * to_log2
            blocks = chunk // BLK
            bias = bias_ref[0, pl.ds(c * blocks, blocks), :, lanes]
            s = (s.reshape(blocks, BLK, row_tile) + bias).reshape(chunk, row_tile)
            s_buf[pl.ds(c * chunk, chunk)] = s
            return jnp.maximum(top, jnp.max(s, axis=0, keepdims=True))

        top = for_chunks(count, score_step, jnp.full((1, row_tile), -jnp.inf, jnp.float32))

        def weight_step(c, carry):
            total, out_t = carry
            e = jnp.exp2(s_buf[pl.ds(c * chunk, chunk)] - top)
            total = total + jnp.sum(e, axis=0, keepdims=True)
            e16 = e.astype(jnp.bfloat16)
            e_buf[pl.ds(c * chunk, chunk)] = e16
            out_t = out_t + dot(kv_chunk(1, c).T, e16)
            return total, out_t

        total, out_t = for_chunks(
            count,
            weight_step,
            (jnp.zeros((1, row_tile), jnp.float32), jnp.zeros((width, row_tile), jnp.float32)),
        )
        inverse = 1.0 / total
        out16 = (out_t * inverse).T.astype(jnp.bfloat16)
        out32 = out16.astype(jnp.float32)
        out_ref[pl.ds(t0, tile_tokens)] = out32.reshape(tile_tokens, group, width).astype(jnp.bfloat16)
        delta = jnp.sum((g32 * out32).T, axis=0, keepdims=True) * inverse
        g16 = (g32.T * inverse).T.astype(jnp.bfloat16)

        def grad_step(c, dq_t):
            at = pl.ds(c * chunk, chunk)
            e16 = e_buf[at]
            dp = dot(kv_chunk(1, c), g16, NT)
            ds = (e16.astype(jnp.float32) * (dp - delta)).astype(jnp.bfloat16)
            dk = dot(ds, q)
            dv = dot(e16, g16)
            if tile > 0:
                dk = dk + acc[0, at]
                dv = dv + acc[1, at]
            if tile < tiles - 1:
                acc[0, at] = dk
                acc[1, at] = dv
            else:
                shape = (per_chunk, shard_tokens, width)
                spot = pl.ds(c * per_chunk, per_chunk)
                dkv_ref[spot, 0, 0] = (dk * factor).astype(jnp.bfloat16).reshape(shape)
                dkv_ref[spot, 0, 1] = dv.astype(jnp.bfloat16).reshape(shape)
            return dq_t + dot(kv_chunk(0, c).T, ds)

        dq_t = for_chunks(count, grad_step, jnp.zeros((width, row_tile), jnp.float32))
        dq = (dq_t * factor).T.reshape(tile_tokens, group, width)
        dq_ref[pl.ds(t0, tile_tokens)] = dq.astype(jnp.bfloat16)


def local_attention(queries, out_grad, kv, bias):
    tokens, heads, width = queries.shape
    shards, kv_heads, _, shard_tokens, _ = kv.shape
    group = heads // kv_heads
    length = shards * shard_tokens
    rows = tokens * group
    chunk = math.gcd(length, 256)
    row_tile = rows
    while row_tile * length > (1 << 21) and row_tile > 128:
        row_tile //= 2
    acc_rows = length if row_tile < rows else 8
    blocks = length // BLK
    q_spec = pl.BlockSpec((tokens, group, width), lambda g: (0, g, 0))
    kv_spec = pl.BlockSpec((shards, 1, 2, shard_tokens, width), lambda g: (0, g, 0, 0, 0))
    return pl.pallas_call(
        functools.partial(attention, (chunk, row_tile)),
        grid=(kv_heads,),
        in_specs=[
            q_spec,
            q_spec,
            kv_spec,
            pl.BlockSpec((1, blocks, 1, rows), lambda g: (g, 0, 0, 0)),
        ],
        out_specs=[q_spec, q_spec, kv_spec],
        out_shape=[
            jax.ShapeDtypeStruct(queries.shape, jnp.bfloat16),
            jax.ShapeDtypeStruct(queries.shape, jnp.bfloat16),
            jax.ShapeDtypeStruct(kv.shape, jnp.bfloat16),
        ],
        scratch_shapes=[
            pltpu.VMEM((length, row_tile), jnp.float32),
            pltpu.VMEM((length, row_tile), jnp.bfloat16),
            pltpu.VMEM((2, acc_rows, width), jnp.float32),
        ],
        compiler_params=pltpu.CompilerParams(vmem_limit_bytes=60 * 1024 * 1024),
        name="attention",
    )(queries, out_grad, kv, bias)


def row_bias(rand_all, global_blocks, first, here, block_count, kv_heads):
    heads = rand_all.shape[0]
    group = heads // kv_heads
    mine = lax.dynamic_slice_in_dim(rand_all, first, here, axis=1)
    ids = first + jnp.arange(here, dtype=jnp.int32)
    key_ids = jnp.arange(block_count, dtype=jnp.int32)
    away = (key_ids[None, :] - ids[:, None] + block_count + 1) % block_count
    common = (away <= 2) | jnp.any(key_ids[None, :, None] == global_blocks[None, None, :], axis=2)
    chosen = jnp.any(mine[:, :, None, :] == key_ids[None, None, :, None], axis=3)
    live = chosen | common[None]
    bias = jnp.where(live, 0.0, -jnp.inf).astype(jnp.float32)
    bias = bias.reshape(kv_heads, group, here, block_count).transpose(0, 3, 2, 1)
    bias = jnp.broadcast_to(bias[:, :, :, None, :], (kv_heads, block_count, here, BLK, group))
    return bias.reshape(kv_heads, block_count, 1, here * BLK * group)


def fused_kernel(
    rand_in, glob_in, k_in, v_in, q_hbm, g_hbm, out_ref, dq_ref, dk_ref, dv_ref,
    grads_ref, kv_in, q_buf, g_buf, kv_buf, part_buf, sib_in, right_in, left_in, right_out, left_out,
    ids_out, ids_buf, mark_buf, coarse_k, coarse_q, e_buf, ds_buf, vt_buf, kt_buf, qt_buf, gt_buf,
    in_sem, q_sem, g_sem,
    ids_send, sib_send, fwd_send, back_send, far_send, pair_send, right_send, left_send,
    ids_recv, sib_recv, kv_recv, pair_recv, right_recv, left_recv,
):
    heads, _, chips, _, shard_tokens, width = kv_buf.shape
    shards = 2 * chips
    _, tokens, group, _ = q_buf.shape
    rows = tokens * group
    here = tokens // BLK
    block_count = shards * here
    lane_keys = chips * shard_tokens
    tile = 256
    tiles = rows // tile
    tile_tokens = tile // group
    chunk = 2 * shard_tokens
    chunks = shards * shard_tokens // chunk
    factor = 1.0 / math.sqrt(width)
    to_log2 = factor * math.log2(math.e)
    me = lax.axis_index("ctx")
    z, core = me // 2, me % 2
    pair = z * 2 + 1 - core
    ahead, behind = me + 2, me - 2
    last = chips - 1

    barrier = pltpu.get_barrier_semaphore()
    for k in range(1, shards):
        pl.semaphore_signal(
            barrier, inc=1, device_id={"ctx": lax.rem(me + k, shards)}, device_id_type=pl.DeviceIdType.MESH
        )

    def send(source, target, send_sem, recv_sem, to):
        return pltpu.make_async_remote_copy(
            src_ref=source, dst_ref=target, send_sem=send_sem, recv_sem=recv_sem,
            device_id={"ctx": to}, device_id_type=pl.DeviceIdType.MESH,
        )

    def send_ids(k):
        to = lax.rem(me + k, shards)
        return send(ids_out.at[to], ids_buf.at[me], ids_send, ids_recv.at[me], to)

    def got_ids(k):
        origin = lax.rem(me + k, shards)
        return send(ids_out.at[origin], ids_buf.at[origin], ids_send, ids_recv.at[origin], origin)

    def kv_spot(h, origin, w):
        return kv_buf.at[h, core, origin] if w is None else kv_buf.at[h, core, origin, w]

    def kv_move(h, origin, send_sem, to, w=None):
        spot = kv_spot(h, origin, w)
        return send(spot, spot, send_sem, kv_recv.at[heads if w == 1 else h, origin], to)

    def right_kv(h, origin, w=None):
        return kv_move(h, origin, fwd_send, ahead, w)

    def left_kv(h, origin, w=None):
        return kv_move(h, origin, back_send, behind, w)

    def sib_kv(h, origin, w=None):
        spot = kv_spot(h, origin, w)
        return send(spot, spot, sib_send, sib_recv.at[h], pair)

    def pair_move(h, w):
        return send(part_buf.at[h, w, 1 - core], sib_in.at[h, w], pair_send, pair_recv.at[h, w], pair)

    def side_move(side, h, zd, w=None):
        out, arrived = (right_out, right_in) if side == 0 else (left_out, left_in)
        sems = (right_send, right_recv) if side == 0 else (left_send, left_recv)
        at, slot = (h, zd), h
        if w is not None:
            at, slot = (h, zd, w), h + w
        return send(out.at[at], arrived.at[at], sems[0], sems[1].at[slot, zd], ahead if side == 0 else behind)

    def head_columns(ref, h):
        return ref.at[:, pl.ds(pl.multiple_of(h * group, group), group), :]

    def load_q(h):
        return pltpu.make_async_copy(head_columns(q_hbm, h), q_buf.at[h], q_sem.at[h])

    def load_g(h):
        return pltpu.make_async_copy(head_columns(g_hbm, h), g_buf.at[h], g_sem.at[h])

    def each_head(step):
        def run(h, carry):
            step(h)
            return carry
        lax.fori_loop(0, heads, run, 0)

    loads = [pltpu.make_async_copy(ref, kv_in.at[which], in_sem.at[which]) for which, ref in enumerate((k_in, v_in))]
    for load in loads:
        load.start()


    slots = rand_in.shape[0]
    lanes = ids_buf.shape[2]
    spread = lax.broadcasted_iota(jnp.int32, (group, lanes), 1) % group
    spread = (spread == lax.broadcasted_iota(jnp.int32, (group, lanes), 0)).astype(jnp.float32)
    for k in range(slots):
        picks = lax.dot_general(
            rand_in[k].astype(jnp.float32), spread, (((0,), (0,)), ((), ())), preferred_element_type=jnp.float32
        )
        for to in range(shards):
            for b in range(here):
                spot = to * here + b
                ids_out[to, b * slots + k:b * slots + k + 1] = picks[spot:spot + 1]
    ids_buf[me] = ids_out[me]

    for which, load in enumerate(loads):
        load.wait()
        turned = jnp.swapaxes(kv_in[which].astype(jnp.float32), 0, 1)
        kv_buf[:, core, z, which] = turned.astype(jnp.bfloat16)

    pl.semaphore_wait(barrier, shards - 1)

    def own_right(h, w=None):
        @pl.when(z < last)
        def _():
            right_kv(h, z, w).start()

    def own_left(h, w=None):
        @pl.when(z > 0)
        def _():
            left_kv(h, z, w).start()

    def own_sib(h):
        sib_kv(h, z).start()

    ends = jnp.logical_or(z == 0, z == last)
    middle = jnp.logical_not(ends)

    def landed(h, origin, w=None):
        kv_move(h, origin, fwd_send, pair, w).wait_recv()

    def end_arrive(h, distance, w=None):
        origin = jnp.where(z == 0, distance, last - distance)
        landed(h, origin, w)
        sib_kv(h, origin, w).start()

    def near_arrive(h, w=None):
        landed(h, z - 1, w)
        right_kv(h, z - 1, w).start()
        sib_kv(h, z - 1, w).start()
        landed(h, z + 1, w)
        left_kv(h, z + 1, w).start()
        sib_kv(h, z + 1, w).start()

    def far_arrive(h, w=None):
        origin = jnp.where(z == 1, last, 0)
        landed(h, origin, w)
        kv_move(h, origin, far_send, jnp.where(z == 1, behind, ahead), w).start()
        sib_kv(h, origin, w).start()

    def over(low, high, step):
        def run(h, carry):
            step(h)
            return carry
        lax.fori_loop(low, high, run, 0)

    def combined(h, zd, w=None):
        at = slice(None) if w is None else w
        return part_buf[h, at, core, zd].astype(jnp.float32) + sib_in[h, at, zd].astype(jnp.float32)

    def reduce(rank, h, w=None, only=None):
        for side in range(2):
            zz = rank if side == 0 else last - rank
            targets = list(range(last, zz, -1) if side == 0 else range(zz))
            if only is not None:
                targets = targets[only:only + 1]
            out, arrived = (right_out, right_in) if side == 0 else (left_out, left_in)

            @pl.when(z == zz)
            def _(side=side, targets=targets, out=out, arrived=arrived):
                for zd in targets:
                    at = (h, zd) if w is None else (h, zd, w)
                    total = combined(h, zd, w)
                    if rank > 0:
                        side_move(side, h, zd, w).wait_recv()
                        total = total + arrived[at].astype(jnp.float32)
                    out[at] = total.astype(jnp.bfloat16)
                    side_move(side, h, zd, w).start()

    def finish(h, w=None):
        for zz in range(chips):
            @pl.when(z == zz)
            def _(zz=zz):
                at = (h, zz) if w is None else (h, zz, w)
                total = combined(h, zz, w)
                if zz > 0:
                    side_move(0, h, zz, w).wait_recv()
                    total = total + right_in[at].astype(jnp.float32)
                if zz < last:
                    side_move(1, h, zz, w).wait_recv()
                    total = total + left_in[at].astype(jnp.float32)
                for which in range(2) if w is None else (w,):
                    piece = total[which] if w is None else total
                    grads_ref[h, which] = piece.T.astype(jnp.bfloat16)

    def compute(h, hooks):
        load_q(h).wait()
        load_g(h).wait()
        ids = ids_buf[h]
        key_ids = lax.broadcasted_iota(jnp.int32, (block_count, lanes), 0)
        key_float = key_ids.astype(jnp.float32)
        for b in range(here):
            away = key_ids - (me * here + b) + (block_count + 1)
            for _ in range(2):
                away = jnp.where(away >= block_count, away - block_count, away)
            live = (away <= 2) | (key_ids == glob_in[0]) | (key_ids == glob_in[1])
            for k in range(slots):
                live = live | (key_float == ids[b * slots + k:b * slots + k + 1])
            bias = jnp.where(live, 0.0, HIDDEN).astype(jnp.float32).astype(jnp.bfloat16)
            half = rows // here
            qt_buf[width:width + block_count, b * half:(b + 1) * half] = jnp.concatenate([bias] * (half // lanes), axis=1)
            hide = jnp.where(live, 0.0, -COARSE_MAX).astype(jnp.float32)
            hide = jnp.concatenate([hide, jnp.zeros((32 - block_count, lanes), jnp.float32)], axis=0).astype(COARSE)
            coarse_q[width:width + 32, b * half:(b + 1) * half] = jnp.concatenate([hide] * (half // lanes), axis=1)

        def key_rows(which, c):
            lane, zz = c * chunk // lane_keys, c * chunk % lane_keys // shard_tokens
            return kv_buf[h, lane, zz:zz + 2, which].reshape(chunk, width)

        def columns(r):
            return slice(r * tile, (r + 1) * tile)

        def keys_at(c):
            return slice(c * chunk, (c + 1) * chunk)

        def turned_rows(ref, r):
            return ref[h, r * tile_tokens:(r + 1) * tile_tokens].reshape(tile, width).T

        def put_rows(ref, r, turned):
            block = turned.T.reshape(tile_tokens, group, width)
            ref[r * tile_tokens:(r + 1) * tile_tokens, pl.ds(pl.multiple_of(h * group, group), group), :] = block

        tops = {}

        def turn_keys(which, ref):
            for c in range(chunks):
                ref[:width, keys_at(c)] = key_rows(which, c).T

        def marked(which, at):
            size, spot = at.stop - at.start, at.start
            lane, zz = spot // lane_keys, spot % lane_keys // shard_tokens
            keys = kv_buf[h, lane, zz:zz + size // shard_tokens, which].reshape(size, width)
            return jnp.concatenate([keys, mark_buf[at]], axis=1)

        def slabs(size):
            return [slice(at, at + size) for at in range(0, length, size)]

        def coarse_keys():
            for c in range(chunks):
                coarse_k[keys_at(c), :width] = key_rows(0, c).astype(jnp.float32).astype(COARSE)

        def scores(r):
            qt = turned_rows(q_buf, r)
            qt_buf[:width, columns(r)] = qt
            coarse_q[:width, columns(r)] = qt.astype(jnp.float32).astype(COARSE)
            right = coarse_q[:, columns(r)]
            top = None
            for at in slabs(512):
                high = jnp.max(dot(coarse_k[at], right).reshape(512 // 8, 8, tile), axis=0)
                top = high if top is None else jnp.maximum(top, high)
            tops[r] = jnp.max(top, axis=0, keepdims=True) * to_log2

        def weights(r):
            right = qt_buf[:, columns(r)]
            for at in slabs(512):
                e = jnp.exp2(dot(marked(0, at), right) * to_log2 - tops[r])
                e_buf[at, columns(r)] = e.astype(jnp.bfloat16)

        def outputs(r):
            out_t = dot(vt_buf[...], e_buf[:, columns(r)])
            inverse = 1.0 / out_t[width:width + 1]
            out16 = (out_t[:width] * inverse).astype(jnp.bfloat16)
            gt = turned_rows(g_buf, r).astype(jnp.float32)
            rest = jnp.sum(gt * out16.astype(jnp.float32), axis=0, keepdims=True) * -inverse
            gt_buf[:width, columns(r)] = (gt * inverse).astype(jnp.bfloat16)
            level = lax.broadcasted_iota(jnp.int32, (16, tile), 0)
            split = jnp.zeros((16, tile), jnp.float32)
            for k in range(3):
                part = rest.astype(jnp.bfloat16).astype(jnp.float32)
                split = jnp.where(level == k, part, split)
                rest = rest - part
            gt_buf[width + block_count:width + block_count + 16, columns(r)] = split.astype(jnp.bfloat16)
            put_rows(out_ref, r, out16)

        def score_grads(r):
            right = gt_buf[:, columns(r)]
            for at in slabs(512):
                dp = dot(marked(1, at), right).astype(jnp.bfloat16)
                ds_buf[at, columns(r)] = e_buf[at, columns(r)] * dp

        def query_grads(r):
            dq_t = dot(kt_buf[...], ds_buf[:, columns(r)]) * factor
            put_rows(dq_ref, r, dq_t.astype(jnp.bfloat16))

        def key_grads(lane, w):
            left, right = ((qt_buf, ds_buf), (gt_buf, e_buf))[w]
            for zz in range(0, chips, 2):
                at = pl.ds(pl.multiple_of(lane * lane_keys + zz * shard_tokens, chunk), chunk)
                grad = dot(left[:width], right[at], NT)
                if w == 0:
                    grad = grad * factor
                grad = grad.astype(jnp.bfloat16)
                for j in range(2):
                    part_buf[h, w, lane, zz + j] = grad[:, j * shard_tokens:(j + 1) * shard_tokens]

        turn_keys(1, vt_buf)
        coarse_keys()
        scores(0)
        scores(1)
        weights(0)
        scores(2)
        weights(1)
        outputs(0)
        scores(3)
        weights(2)
        outputs(1)
        turn_keys(0, kt_buf)
        weights(3)
        outputs(2)
        outputs(3)
        key_grads(1 - core, 1)
        pair_move(h, 1).start()
        for r in range(tiles):
            score_grads(r)
        hooks[0]()
        key_grads(1 - core, 0)
        pair_move(h, 0).start()
        for r in range(tiles):
            query_grads(r)
        key_grads(core, 1)
        key_grads(core, 0)

    def lead(rank, t):
        return jnp.where(rank == 0, heads, jnp.minimum(jnp.where(rank == 1, 3 + 2 * t, 2 + t), heads))

    def start_loads(h):
        load_q(h).start()
        load_g(h).start()

    for w in range(2):
        own_right(0, w)
        own_left(0, w)
    for h in range(3):
        own_sib(h)
    for k in range(1, shards):
        send_ids(k).start()

    @pl.when(z == 0)
    def _():
        over(1, heads, own_right)

    @pl.when(z == last)
    def _():
        over(1, heads, own_left)
    each_head(start_loads)

    length = shards * shard_tokens
    spot = lax.broadcasted_iota(jnp.int32, (length, width), 0)
    spot_lane, spot_chip = spot // lane_keys, spot % lane_keys // shard_tokens
    spot_block = (spot_chip * 2 + spot_lane) * here + spot % shard_tokens // BLK
    column = lax.broadcasted_iota(jnp.int32, (length, width), 1)
    ones = jnp.logical_and(column >= block_count, column < block_count + 3)
    mark_buf[...] = jnp.logical_or(column == spot_block, ones).astype(jnp.float32).astype(jnp.bfloat16)
    coarse_k[:, width:] = jnp.where(column == spot_block, COARSE_MAX, 0.0).astype(COARSE)
    coarse_q[width:, :] = jnp.zeros((width, rows), jnp.float32).astype(COARSE)
    vt_buf[width:, :] = jnp.ones((16, length), jnp.bfloat16)
    qt_buf[width:, :] = jnp.zeros((width, rows), jnp.bfloat16)
    gt_buf[width:, :] = jnp.zeros((width, rows), jnp.bfloat16)

    @pl.when(middle)
    def _():
        near_arrive(0, 0)
        near_arrive(0, 1)
        right_kv(1, z).start()
        left_kv(1, z).start()
        far_arrive(0, 0)
        far_arrive(0, 1)
        near_arrive(1)

    over(jnp.where(ends, heads, 2), lead(z, 0), own_right)
    over(jnp.where(ends, heads, 2), lead(last - z, 0), own_left)

    @pl.when(ends)
    def _():
        for distance in range(1, chips):
            end_arrive(0, distance, 0)
            end_arrive(0, distance, 1)

    for k in range(1, shards):
        got_ids(k).wait_recv()

    final = heads - 1

    def near_done(t):
        return jnp.minimum(jnp.minimum(2 + 2 * t, 4 + t), heads)

    def slot(t, carry):
        over(lead(z, t), lead(z, t + 1), own_right)
        over(lead(last - z, t), lead(last - z, t + 1), own_left)

        @pl.when(t + 3 < heads)
        def _():
            own_sib(t + 3)

        @pl.when(jnp.logical_and(middle, t == 1))
        def _():
            far_arrive(2)

        send(kv_buf.at[t, 1 - core], kv_buf.at[t, 1 - core], sib_send, sib_recv.at[t], pair).wait_recv()

        def hook():
            @pl.when(jnp.logical_and(ends, t < final))
            def _():
                for distance in range(1, chips):
                    end_arrive(t + 1, distance)

            @pl.when(middle)
            def _():
                far = jnp.where(t == 0, 1, t + 2)
                over(far, jnp.minimum(far + 1, heads), far_arrive)
                over(near_done(t), near_done(t + 1), near_arrive)

            @pl.when(t > 0)
            def _():
                pair_move(t - 1, 1).wait_recv()
                pair_move(t - 1, 0).wait_recv()
                reduce(0, t - 1)

            @pl.when(t > 1)
            def _():
                reduce(1, t - 2)

            low = jnp.where(t == final - 1, 0, t - 3)
            over(low, jnp.where(t < final - 1, low, t - 2), lambda h: reduce(2, h))

        compute(t, [hook])
        return carry

    lax.fori_loop(0, heads, slot, 0)

    reduce(1, final - 1)
    reduce(2, final - 2)
    reduce(2, final - 1)
    pair_move(final, 1).wait_recv()
    reduce(0, final, 1, 0)
    pair_move(final, 0).wait_recv()
    for rank, w, only in ((0, 0, 0), (0, 1, 1), (0, 0, 1), (0, 1, 2), (0, 0, 2),
                          (1, 1, 0), (1, 0, 0), (2, 1, 0), (1, 1, 1), (2, 0, 0), (1, 0, 1)):
        reduce(rank, final, w, only)
    over(0, final, finish)
    finish(final, 1)
    finish(final, 0)

    for which, ref in enumerate((dk_ref, dv_ref)):
        turned = jnp.swapaxes(grads_ref[:, which].astype(jnp.float32), 0, 1)
        ref[...] = turned.astype(jnp.bfloat16)

    def drained(region, sem):
        send(region, region, sem, ids_recv.at[0], pair).wait_send()

    drained(ids_out.at[pl.ds(1, shards - 1)], ids_send)
    drained(kv_buf.at[:, 0], sib_send)
    drained(sib_in, pair_send)
    @pl.when(middle)
    def _():
        drained(kv_buf.at[:, 0, pl.ds(0, 2)], fwd_send)
        drained(kv_buf.at[:, 0, pl.ds(0, 2)], back_send)
        drained(kv_buf.at[:, 0, 0], far_send)

    for zz in range(chips):
        @pl.when(z == zz)
        def _(zz=zz):
            if zz == 0:
                drained(kv_buf.at[:, 0, 0], fwd_send)
            if zz == last:
                drained(kv_buf.at[:, 0, 0], back_send)
            if zz < last:
                drained(right_out.at[:, pl.ds(0, last - zz)], right_send)
            if zz > 0:
                drained(left_out.at[:, pl.ds(0, zz)], left_send)


def fused(queries, out_grad, keys, values, rand_blocks, global_blocks, shards):
    tokens, heads, width = queries.shape
    kv_heads = keys.shape[1]
    group = heads // kv_heads
    chips = shards // 2
    rows = tokens * group
    length = tokens * shards
    blocks = length // BLK
    here = tokens // BLK
    bf16, f32 = jnp.bfloat16, jnp.float32
    vmem = pl.BlockSpec(memory_space=pltpu.VMEM)
    smem = pl.BlockSpec(memory_space=pltpu.SMEM)
    anywhere = pl.BlockSpec(memory_space=pl.ANY)
    dma = pltpu.SemaphoreType.DMA
    piece = (2, tokens, width)
    block = pltpu.VMEM((kv_heads, tokens, group, width), bf16)
    hop = pltpu.VMEM((kv_heads, chips, 2, width, tokens), bf16)
    gift = pltpu.VMEM((kv_heads, 2, chips, width, tokens), bf16)
    results = pl.pallas_call(
        fused_kernel,
        in_specs=[vmem, smem] + [anywhere] * 4,
        out_specs=[vmem] * 4,
        out_shape=[
            pltpu.VMEM(queries.shape, bf16),
            pltpu.VMEM(queries.shape, bf16),
            pltpu.VMEM(keys.shape, bf16),
            pltpu.VMEM(keys.shape, bf16),
        ],
        scratch_shapes=[pltpu.VMEM((kv_heads,) + piece, bf16), pltpu.VMEM((2,) + keys.shape, bf16)] + [block] * 2
        + [
            pltpu.VMEM((kv_heads, 2, chips) + piece, bf16),
            pltpu.VMEM((kv_heads, 2, 2, chips, width, tokens), bf16),
        ]
        + [gift]
        + [hop] * 4
        + [
            pltpu.VMEM((shards, 8, 128), f32),
            pltpu.VMEM((shards, 8, 128), f32),
            pltpu.VMEM((length, 128), bf16),
            pltpu.VMEM((length, 2 * width), COARSE),
            pltpu.VMEM((2 * width, rows), COARSE),
            pltpu.VMEM((length, rows), bf16),
            pltpu.VMEM((length, rows), bf16),
            pltpu.VMEM((width + 16, length), bf16),
            pltpu.VMEM((width, length), bf16),
            pltpu.VMEM((2 * width, rows), bf16),
            pltpu.VMEM((2 * width, rows), bf16),
        ]
        + [dma((2,))]
        + [dma((kv_heads,))] * 2
        + [dma] * 8
        + [dma((shards,)), dma((kv_heads,)), dma((kv_heads + 1, chips)), dma((kv_heads, 2))]
        + [dma((kv_heads + 1, chips))] * 2,
        compiler_params=pltpu.CompilerParams(
            collective_id=0, has_side_effects=True, vmem_limit_bytes=50 * 1024 * 1024,
        ),
        name="fused",
    )(rand_blocks.transpose(2, 0, 1), global_blocks, keys, values, queries, out_grad)
    return settle(results)


def settle(arrays):
    count = len(arrays)

    def kernel(*refs):
        copies = [pltpu.make_async_copy(refs[i], refs[count + i], refs[2 * count].at[i]) for i in range(count)]
        for copy in copies:
            copy.start()
        for copy in copies:
            copy.wait()

    anywhere = pl.BlockSpec(memory_space=pl.ANY)
    return pl.pallas_call(
        kernel,
        in_specs=[pl.BlockSpec(memory_space=pltpu.VMEM)] * count,
        out_specs=[pl.BlockSpec(memory_space=pltpu.HBM)] * count,
        out_shape=[jax.ShapeDtypeStruct(a.shape, a.dtype) for a in arrays],
        scratch_shapes=[pltpu.SemaphoreType.DMA((count,))],
        compiler_params=pltpu.CompilerParams(vmem_limit_bytes=1 << 20),
        name="settle",
    )(*[pltpu.with_memory_space_constraint(a, pltpu.VMEM) for a in arrays])


def body(shards, queries, keys, values, out_grad, rand_blocks, global_blocks):
    tokens, kv_heads, width = keys.shape
    here = tokens // BLK
    block_count = rand_blocks.shape[1]
    group = queries.shape[1] // kv_heads
    me = lax.axis_index("ctx")
    if (shards == kv_heads == group == 8 and here == 2 and rand_blocks.shape[2] == 3
            and global_blocks.shape[0] == 2):
        return fused(queries, out_grad, keys, values, rand_blocks, global_blocks, shards)
    kv_here = jnp.stack([keys.transpose(1, 0, 2), values.transpose(1, 0, 2)], axis=1)
    kv = lax.all_gather(kv_here, "ctx", axis=0)
    rand_all = lax.all_gather(rand_blocks, "ctx", axis=0, tiled=True)
    bias = row_bias(rand_all, global_blocks, me * here, here, block_count, kv_heads)
    output, query_grad, parts = local_attention(queries, out_grad, kv, bias)
    sums = lax.psum_scatter(parts, "ctx", scatter_dimension=0, tiled=False)
    grads = sums.transpose(1, 2, 0, 3)
    return output, query_grad, grads[0], grads[1]


def solution(mesh):
    split = P(("dp", "ctx"), None, None)
    return jax.shard_map(
        functools.partial(body, mesh.shape["ctx"]),
        mesh=mesh,
        in_specs=(split, split, split, split, split, P("dp")),
        out_specs=(split, split, split, split),
        check_vma=False,
    )
```
